32 devices in a mesh: cohort: 2 (over x), region: 16 (over z, y, core).
Axes of the slice: x: 2, y: 2, z: 4, core: 2. Of those that a mesh axis runs over, the one named last changes fastest.
Arguments:
- dosage: bfloat16 [4096, 16384], P('cohort', 'region'), parts along dimension 0, may hold values from 0 to 2, as said below
- eigvec: bfloat16 [16384, 2048], P('region', 'cohort'), parts along dimension 1, may hold values from -1 to 1, as said below
- eigval: float32 [2, 16384], P('cohort', 'region'), parts along dimension 0, may hold values from 64 to 65536
- pheno: bfloat16 [4096, 128], P('cohort'), parts along dimension 0, may hold values from 0 to 1, as said below
Outputs:
- level1_weights: float32 [128, 128], P('region', 'cohort'), parts along dimension 1
The draws below stay inside these ranges and needn't reach their ends.
There are 2 independent parts, one for each index of `cohort`. The reference program is written for one: setup_inputs(seed, part) draws one part's arguments, and reference() takes and returns one part's arrays. A program takes and returns all parts, laid end to end along the dimension named above; each array names one. Nothing has to cross between parts.
Inputs may be any that keep to these rules, and one draw needn't show every extreme that they name: Every entry is a whole dosage 0, 1 or 2. `eigvec`: the rows of each block form an orthonormal basis up to rounding. `pheno`: every entry is 0 or 1.
All inputs are finite; a program needn't handle non-finite values.
Results may differ from the reference program's by a relative error of at most 0.0051.
Values may be sent and summed in bfloat16 or wider, within the bound.
No kernel may reach another device: no remote copies, remote signals or barrier semaphores. Data moves between devices by JAX's collectives and lax.ppermute only.
A program may use at most 64 MiB of HBM per device.

```python
import math
import jax
import jax.numpy as jnp
from jax import lax

BLK = 1024
TRAITS = 128
SAMPLES = 2048
NEWTON = 3
VARIANTS = 16384


def draw_dosage(key, part):
    freq = jax.random.randint(jax.random.fold_in(key, 11), (1, VARIANTS), 100, 501)
    first = jax.random.randint(jax.random.fold_in(key, 12), (SAMPLES, VARIANTS), 0, 1000)
    second = jax.random.randint(jax.random.fold_in(key, 13), (SAMPLES, VARIANTS), 0, 1000)
    count = (first < freq).astype(jnp.int32) + (second < freq).astype(jnp.int32)
    return count.astype(jnp.float32).astype(jnp.bfloat16)


def draw_eigvec(key, part):
    blocks = VARIANTS // BLK
    normal = jax.random.normal(jax.random.fold_in(key, 21), (blocks, BLK, BLK), jnp.float32)
    basis, upper = jnp.linalg.qr(normal)
    return basis.reshape(VARIANTS, BLK).astype(jnp.bfloat16)


def draw_pheno(key, part):
    status = jax.random.randint(jax.random.fold_in(key, 31), (SAMPLES, TRAITS), 0, 2)
    return status.astype(jnp.float32).astype(jnp.bfloat16)


def shard_levels(stream_key, extent, cuts, smallest, largest):
    def one(dim, parts):
        steps = jax.random.uniform(jax.random.fold_in(jax.random.fold_in(stream_key, 6), dim), (parts,), jnp.float32, smallest / len(cuts), largest / len(cuts))
        return jnp.repeat(jnp.exp(steps), extent[dim] // parts).reshape((-1,) + (1,) * (len(extent) - dim - 1))

    loudness = one(*cuts[0])
    for cut in cuts[1:]:
        loudness = loudness * one(*cut)
    return loudness


def setup_inputs(seed: int = 0, part: int = 0) -> dict:
    seeds = jax.random.split(jax.random.key(seed), 5)
    part_splits = jax.random.split(jax.random.fold_in(seeds[4], part), 5)
    dosage = draw_dosage(jax.random.fold_in(jax.random.fold_in(seeds[4], part), 71), part)
    eigvec = draw_eigvec(jax.random.fold_in(jax.random.fold_in(seeds[4], part), 71), part)
    eigval = jnp.clip(jnp.exp(math.log(65536.0) - 6.931472 * jax.random.uniform(part_splits[2], (1, VARIANTS), jnp.float32) ** shard_levels(part_splits[2], (1, VARIANTS), ((1, 16),), -0.2, 0.2)), 64.0, 65536.0)
    pheno = draw_pheno(jax.random.fold_in(jax.random.fold_in(seeds[4], part), 71), part)
    return dict(dosage=dosage, eigvec=eigvec, eigval=eigval, pheno=pheno)


EPSILON = 1e-05
HERITABILITY = (0.01, 0.25, 0.75, 0.99)
LEVEL_ONE = 0.03125

def standardize(values):
    values = values.astype(jnp.float32)
    center = lax.optimization_barrier(jnp.mean(values, axis=0))
    spread = jnp.sqrt(lax.optimization_barrier(jnp.mean(jnp.square(values - center), axis=0)) + EPSILON)
    return ((values - center) / spread).astype(jnp.bfloat16)

def fit_trait(operands):
    design, target = operands
    predictors = design.shape[0]
    level_ridge = LEVEL_ONE * design.shape[1]
    weights = jnp.zeros((predictors,), jnp.float32)
    identity = jnp.eye(predictors, dtype=jnp.float32)
    for newton_step in range(NEWTON):
        logits = jnp.dot(weights.astype(jnp.bfloat16).astype(jnp.float32), design.astype(jnp.float32), preferred_element_type=jnp.float32)
        prob = jax.nn.sigmoid(logits)
        resid = (target - prob).astype(jnp.bfloat16)
        weighted = (design.astype(jnp.float32) * (prob * (1.0 - prob))).astype(jnp.bfloat16)
        gram = jnp.dot(weighted.astype(jnp.float32), design.T.astype(jnp.float32), preferred_element_type=jnp.float32)
        grad = jnp.dot(design.astype(jnp.float32), resid.astype(jnp.float32), preferred_element_type=jnp.float32) - level_ridge * weights
        factor = jnp.linalg.cholesky(gram + level_ridge * identity)
        partial_solve = lax.linalg.triangular_solve(factor, grad[:, None], left_side=True, lower=True)
        update = lax.linalg.triangular_solve(factor, partial_solve, left_side=True, lower=True, transpose_a=True)
        weights = weights + update[:, 0]
    return weights

def reference(dosage, eigvec, eigval, pheno):
    samples = dosage.shape[0]
    blocks = VARIANTS // BLK
    ridges = len(HERITABILITY)
    shrink = jnp.array([BLK * (1.0 - value) / value for value in HERITABILITY], jnp.float32)
    std_trait = standardize(pheno)
    geno_blocks = dosage.reshape(samples, blocks, BLK).transpose(1, 0, 2)
    bases = eigvec.reshape(blocks, BLK, BLK)
    values = eigval.reshape(blocks, BLK)

    def level_zero(operands):
        genotype, basis, spectrum = operands
        std_geno = standardize(genotype)
        cross = lax.dot_general(std_geno.astype(jnp.float32), std_trait.astype(jnp.float32), (((0,), (0,)), ((), ())), preferred_element_type=jnp.float32).astype(jnp.bfloat16)
        rotated = lax.dot_general(basis.astype(jnp.float32), cross.astype(jnp.float32), (((0,), (0,)), ((), ())), preferred_element_type=jnp.float32)
        scaled = (rotated[:, None, :] / (spectrum[:, None, None] + shrink[None, :, None])).astype(jnp.bfloat16)
        ridge = jnp.dot(basis.astype(jnp.float32), scaled.reshape(BLK, ridges * TRAITS).astype(jnp.float32), preferred_element_type=jnp.float32).astype(jnp.bfloat16)
        predicted = lax.dot_general(ridge.astype(jnp.float32), std_geno.astype(jnp.float32), (((0,), (1,)), ((), ())), preferred_element_type=jnp.float32).astype(jnp.bfloat16)
        return predicted.reshape(ridges, TRAITS, samples)
    predictions = lax.map(level_zero, (geno_blocks, bases, values))
    design = predictions.transpose(2, 1, 0, 3).reshape(TRAITS, ridges * blocks, samples)
    target = pheno.astype(jnp.float32).T
    return lax.map(fit_trait, (design, target))
```

```python
import functools

import jax
import jax.numpy as jnp
from jax import lax
from jax.experimental import pallas as pl
from jax.experimental.pallas import tpu as pltpu
from jax.sharding import PartitionSpec as P

NEWTON = 3
EPSILON = 1e-05
HERITABILITY = (0.01, 0.25, 0.75, 0.99)
LEVEL_ONE = 0.03125
RIDGES = len(HERITABILITY)
LANES = 128
TILE = 256


def standardize(values):
    values = values.astype(jnp.float32)
    center = jnp.mean(values, axis=0)
    spread = jnp.sqrt(jnp.mean(jnp.square(values - center), axis=0) + EPSILON)
    return ((values - center) / spread).astype(jnp.bfloat16)


def reorder_matrix(traits, blocks):
    size = blocks * RIDGES * traits
    row = lax.broadcasted_iota(jnp.int32, (size, size), 0)
    column = lax.broadcasted_iota(jnp.int32, (size, size), 1)
    trait, rest = row // (RIDGES * blocks), row % (RIDGES * blocks)
    source = (rest // RIDGES) * (RIDGES * traits) + (rest % RIDGES) * traits + trait
    return jnp.where(column == source, 1.0, 0.0).astype(jnp.bfloat16)


def newton_kernel(traits, predictors, arrived, target, out, design, lhs, system):
    samples = arrived.shape[1]
    blocks = TILE // (RIDGES * traits)
    width = RIDGES * blocks
    order = reorder_matrix(traits, blocks)
    for part in range(arrived.shape[0] // TILE):
        moved = jnp.dot(
            order, arrived[part * TILE : (part + 1) * TILE, :], preferred_element_type=jnp.float32
        ).astype(jnp.bfloat16)
        for t in range(traits):
            start = t * predictors + part * width
            design[start : start + width, :] = moved[t * width : (t + 1) * width]
    level_ridge = LEVEL_ONE * samples
    lane = lax.broadcasted_iota(jnp.int32, (traits, LANES), 1)
    sub = lax.broadcasted_iota(jnp.int32, (traits, LANES), 0)
    row = lax.broadcasted_iota(jnp.int32, (predictors, predictors), 0)
    column = lax.broadcasted_iota(jnp.int32, (predictors, predictors), 1)
    diagonal = jnp.where(row == column, level_ridge, 0.0).astype(jnp.float32)
    fold = LANES // predictors
    pheno = target[...]

    def step(_, weights):
        spread_out = [
            jnp.where(lane // predictors + fold * v == sub, weights, 0.0).astype(jnp.bfloat16)
            for v in range(traits // fold)
        ]
        logits = jnp.dot(
            jnp.concatenate(spread_out, axis=1), design[...], preferred_element_type=jnp.float32
        )
        prob = 1.0 / (1.0 + jnp.exp(-logits))
        curve = prob * (1.0 - prob)
        resid = pheno - prob
        resid = jnp.concatenate([resid, jnp.zeros_like(resid)], axis=0).astype(jnp.bfloat16)
        grad = jnp.zeros((traits, predictors), jnp.float32)
        for t in range(traits):
            own = design[t * predictors : (t + 1) * predictors, :]
            lhs[t, 0:predictors, :] = (own.astype(jnp.float32) * curve[t : t + 1, :]).astype(
                jnp.bfloat16
            )
            lhs[t, predictors : predictors + 2 * traits, :] = resid
            result = lax.dot_general(
                lhs[t], own, (((1,), (1,)), ((), ())), preferred_element_type=jnp.float32
            )
            system[:, t, 0:predictors] = result[0:predictors] + diagonal
            grad = jnp.where(
                sub[:, 0:predictors] == t, result[predictors : predictors + traits], grad
            )
        grad = grad - level_ridge * weights[:, 0:predictors]
        right = jnp.concatenate(
            [
                jnp.broadcast_to(grad[:, i : i + 1], (traits, LANES))[None]
                for i in range(predictors)
            ],
            axis=0,
        )
        table = jnp.where(lane[None] < predictors, system[...], right)
        for k in range(predictors):
            pivot = table[k]
            scaled = (pivot * (1.0 / pivot[:, k : k + 1]))[None]
            below = table - table[:, :, k : k + 1] * scaled
            pieces = [scaled]
            if k > 0:
                pieces = [below[:k]] + pieces
            if k < predictors - 1:
                pieces = pieces + [below[k + 1 :]]
            table = jnp.concatenate(pieces, axis=0)
        for i in range(predictors):
            solved = jnp.broadcast_to(table[i][:, predictors : predictors + 1], (traits, LANES))
            weights = weights + jnp.where(lane % predictors == i, solved, 0.0)
        return weights

    out[...] = lax.fori_loop(0, NEWTON, step, jnp.zeros((traits, LANES), jnp.float32))


def newton(arrived, target):
    rows, samples = arrived.shape
    traits = target.shape[0]
    predictors = rows // traits
    weights = pl.pallas_call(
        functools.partial(newton_kernel, traits, predictors),
        out_shape=jax.ShapeDtypeStruct((traits, LANES), jnp.float32),
        in_specs=[pl.BlockSpec(memory_space=pltpu.VMEM)] * 2,
        out_specs=pl.BlockSpec(memory_space=pltpu.VMEM),
        scratch_shapes=[
            pltpu.VMEM((rows, samples), jnp.bfloat16),
            pltpu.VMEM((traits, predictors + 2 * traits, samples), jnp.bfloat16),
            pltpu.VMEM((predictors, traits, LANES), jnp.float32),
        ],
        compiler_params=pltpu.CompilerParams(vmem_limit_bytes=48 << 20),
        name="newton",
    )(arrived, target)
    return weights[:, :predictors]


def fit_traits(arrived, target):
    rows, samples = arrived.shape
    count = target.shape[0]
    predictors = rows // count
    design = arrived.reshape(-1, RIDGES, count, samples).transpose(2, 0, 1, 3)
    design = design.reshape(count, predictors, samples)
    level_ridge = LEVEL_ONE * samples
    weights = jnp.zeros((count, predictors), jnp.float32)
    identity = jnp.eye(predictors, dtype=jnp.float32)
    for _ in range(NEWTON):
        logits = jnp.einsum(
            "kqn,kq->kn", design, weights.astype(jnp.bfloat16), preferred_element_type=jnp.float32
        )
        prob = jax.nn.sigmoid(logits)
        resid = (target - prob).astype(jnp.bfloat16)
        weighted = (design * (prob * (1.0 - prob))[:, None, :]).astype(jnp.bfloat16)
        gram = jnp.einsum("kqn,kpn->kqp", weighted, design, preferred_element_type=jnp.float32)
        grad = jnp.einsum("kqn,kn->kq", design, resid, preferred_element_type=jnp.float32)
        grad = grad - level_ridge * weights
        factor = jnp.linalg.cholesky(gram + level_ridge * identity)
        partial_solve = lax.linalg.triangular_solve(
            factor, grad[:, :, None], left_side=True, lower=True
        )
        update = lax.linalg.triangular_solve(
            factor, partial_solve, left_side=True, lower=True, transpose_a=True
        )
        weights = weights + update[:, :, 0]
    return weights


def on_device(dosage, eigvec, eigval, pheno):
    samples, width = dosage.shape
    traits = pheno.shape[1]
    regions = lax.axis_size("region")
    per_device = traits // regions
    shrink = jnp.array([width * (1.0 - value) / value for value in HERITABILITY], jnp.float32)
    std_trait = standardize(pheno)
    std_geno = standardize(dosage)
    cross = lax.dot_general(
        std_trait, std_geno, (((0,), (0,)), ((), ())), preferred_element_type=jnp.float32
    ).astype(jnp.bfloat16)
    rotated = jnp.dot(cross, eigvec, preferred_element_type=jnp.float32)
    scaled = rotated.reshape(regions, 1, per_device, width) / (
        eigval[0][None, None, None, :] + shrink[None, :, None, None]
    )
    scaled = scaled.astype(jnp.bfloat16).reshape(RIDGES * traits, width)
    ridge = lax.dot_general(
        scaled, eigvec, (((1,), (1,)), ((), ())), preferred_element_type=jnp.float32
    ).astype(jnp.bfloat16)
    predicted = lax.dot_general(
        ridge, std_geno, (((1,), (1,)), ((), ())), preferred_element_type=jnp.float32
    ).astype(jnp.bfloat16)
    arrived = lax.all_to_all(predicted, "region", split_axis=0, concat_axis=0, tiled=True)
    position = lax.axis_index("region")
    target = lax.dynamic_slice_in_dim(pheno, position * per_device, per_device, 1)
    target = target.astype(jnp.float32).T
    predictors = RIDGES * regions
    if per_device == 8 and LANES % predictors == 0 and predictors < LANES:
        weights = newton(arrived, target)
    else:
        weights = fit_traits(arrived, target)
    weights = weights.reshape(per_device, regions, RIDGES).swapaxes(1, 2)
    return weights.reshape(per_device, predictors)


def solution(mesh):
    return jax.shard_map(
        on_device,
        mesh=mesh,
        in_specs=(
            P("cohort", "region"),
            P("region", "cohort"),
            P("cohort", "region"),
            P("cohort", None),
        ),
        out_specs=P("region", "cohort"),
        check_vma=False,
    )
```

```python
import functools

import jax
import jax.numpy as jnp
from jax import lax
from jax.experimental import pallas as pl
from jax.experimental.pallas import tpu as pltpu
from jax.sharding import PartitionSpec as P

NEWTON = 3
EPSILON = 1e-05
HERITABILITY = (0.01, 0.25, 0.75, 0.99)
LEVEL_ONE = 0.03125
RIDGES = len(HERITABILITY)
LANES = 128
SUBLANES = 8
TILE = 256


def standardize(values):
    values = values.astype(jnp.float32)
    center = jnp.mean(values, axis=0)
    spread = jnp.sqrt(jnp.mean(jnp.square(values - center), axis=0) + EPSILON)
    return ((values - center) / spread).astype(jnp.bfloat16)


def reorder_matrix(traits, blocks, parts):
    size = blocks * RIDGES * traits // parts
    row = lax.broadcasted_iota(jnp.int32, (size, size), 0)
    column = lax.broadcasted_iota(jnp.int32, (size, size), 1)
    group = blocks // parts
    block, rest = row % group, row // group
    ridge, pair = rest % RIDGES, rest // RIDGES
    trait = (pair % 2) * (traits // 2) + pair // 2
    return jnp.where(column == (block * RIDGES + ridge) * traits + trait, 1.0, 0.0).astype(
        jnp.bfloat16
    )


def inverse_two(m):
    (a, b), (c, d) = m
    scale = 1.0 / (a * d - b * c)
    return ((d * scale, -b * scale), (-c * scale, a * scale))


def product(x, y):
    return tuple(
        tuple(x[i][0] * y[0][j] + x[i][1] * y[1][j] for j in range(2)) for i in range(2)
    )


def negative(x):
    return tuple(tuple(-value for value in row) for row in x)


def inverse_four(m):
    def corner(i, j):
        return ((m[i][j], m[i][j + 1]), (m[i + 1][j], m[i + 1][j + 1]))

    first = inverse_two(corner(0, 0))
    left = product(corner(2, 0), first)
    right = product(first, corner(0, 2))
    inner = product(left, corner(0, 2))
    last = corner(2, 2)
    second = inverse_two(
        tuple(tuple(last[i][j] - inner[i][j] for j in range(2)) for i in range(2))
    )
    below = product(second, left)
    back = product(right, below)
    top = tuple(tuple(first[i][j] + back[i][j] for j in range(2)) for i in range(2))
    beside, below = negative(product(right, second)), negative(below)
    return [list(top[i]) + list(beside[i]) for i in range(2)] + [
        list(below[i]) + list(second[i]) for i in range(2)
    ]


def gather_lanes(tile, lanes):
    return jnp.take_along_axis(tile, lanes, axis=1)


def solve(table, span):
    heights, tiles = len(table), len(table[0])
    lane = lax.broadcasted_iota(jnp.int32, (SUBLANES, LANES), 1)
    within = lane % span
    for k in range(0, (tiles - 1) * SUBLANES, 4):
        home, low = k // span, k % span
        first, sub = k // SUBLANES, k % SUBLANES
        rows = [
            [gather_lanes(table[home][r], (lane - within) + low + m) for r in range(first, tiles)]
            for m in range(4)
        ]
        columns = [
            [
                jnp.broadcast_to(table[h][first][sub + m : sub + m + 1], (SUBLANES, LANES))
                for h in range(heights)
            ]
            for m in range(4)
        ]
        pivot = [
            [
                jnp.broadcast_to(rows[m][0][sub + n : sub + n + 1], (SUBLANES, LANES))
                for n in range(4)
            ]
            for m in range(4)
        ]
        inverse = inverse_four(pivot)
        chosen = (within >= low) & (within < low + 4)
        for h in range(heights):
            factors = []
            for n in range(4):
                factor = (columns[0][h] * inverse[0][n] + columns[1][h] * inverse[1][n]) + (
                    columns[2][h] * inverse[2][n] + columns[3][h] * inverse[3][n]
                )
                if h == home:
                    for m in range(4):
                        factor = jnp.where(within == low + m, -inverse[m][n], factor)
                factors.append(factor)
            for r in range(first, tiles):
                base = table[h][r]
                if h == home:
                    base = jnp.where(chosen, 0.0, base)
                table[h][r] = (
                    base
                    - (factors[0] * rows[0][r - first] + factors[1] * rows[1][r - first])
                    - (factors[2] * rows[2][r - first] + factors[3] * rows[3][r - first])
                )
    return [table[h][tiles - 1] for h in range(heights)]


def exchange(tiles, span):
    lane = lax.broadcasted_iota(jnp.int32, (SUBLANES, LANES), 1)
    tiles = list(tiles)
    for bit in (1, 2):
        shift = bit * span
        odd = (lane // shift) % 2 == 1
        for i in range(4):
            if not i & bit:
                x, y = tiles[i], tiles[i | bit]
                tiles[i] = jnp.where(odd, pltpu.roll(y, shift, 1), x)
                tiles[i | bit] = jnp.where(odd, y, pltpu.roll(x, LANES - shift, 1))
    return tiles


def newton_kernel(traits, blocks, arrived, target, out, design, lhs):
    samples = arrived.shape[1]
    predictors = RIDGES * blocks
    half = traits // 2
    parts = arrived.shape[0] // TILE
    order = reorder_matrix(traits, blocks, parts)
    group = blocks // parts
    for part in range(parts):
        moved = jnp.dot(
            order, arrived[part * TILE : (part + 1) * TILE, :], preferred_element_type=jnp.float32
        )
        for i in range(TILE // group):
            start = i * blocks + part * group
            design[start : start + group, :] = moved[i * group : (i + 1) * group].astype(
                jnp.bfloat16
            )
    level_ridge = LEVEL_ONE * samples
    lane = lax.broadcasted_iota(jnp.int32, (SUBLANES, LANES), 1)
    sub = lax.broadcasted_iota(jnp.int32, (SUBLANES, LANES), 0)
    upper = lane >= predictors
    pheno = target[...]
    middle = predictors + 2 * traits

    def step(_, weights):
        spread_out = [
            jnp.where((lane // predictors) * half + s == sub, w, 0.0).astype(jnp.bfloat16)
            for s, w in enumerate(exchange(weights, blocks))
        ]
        logits = jnp.dot(
            jnp.concatenate(spread_out, axis=1), design[...], preferred_element_type=jnp.float32
        )
        prob = 1.0 / (1.0 + jnp.exp(-logits))
        curve = prob * (1.0 - prob)
        resid = pheno - prob
        resid = jnp.concatenate([resid, jnp.zeros_like(resid)], axis=0).astype(jnp.bfloat16)
        found = []
        for s in range(half):
            base = s * 2 * predictors
            for start, trait, place in ((0, s, 0), (predictors, s + half, middle)):
                own = design[base + start : base + start + predictors, :].astype(jnp.float32)
                lhs[s, place : place + predictors, :] = (own * curve[trait : trait + 1, :]).astype(
                    jnp.bfloat16
                )
            lhs[s, predictors:middle, :] = resid
            result = lax.dot_general(
                lhs[s],
                design[base : base + 2 * predictors, :],
                (((1,), (1,)), ((), ())),
                preferred_element_type=jnp.float32,
            )
            tiles = [
                jnp.where(
                    upper,
                    result[middle + SUBLANES * r : middle + SUBLANES * (r + 1)],
                    result[SUBLANES * r : SUBLANES * (r + 1)],
                )
                for r in range(predictors // SUBLANES)
            ]
            first, second = predictors + s, predictors + s + half
            tiles.append(
                jnp.where(
                    upper[:1], result[second : second + 1], result[first : first + 1]
                )
                + jnp.zeros((SUBLANES, LANES), jnp.float32)
            )
            found.append(tiles)
        table = [[] for _ in range(RIDGES)]
        for r in range(predictors // SUBLANES + 1):
            for h, tile in enumerate(exchange([found[s][r] for s in range(half)], blocks)):
                if r < predictors // SUBLANES:
                    same = SUBLANES * r + sub == h * blocks + lane % blocks
                    tile = tile + jnp.where(same, level_ridge, 0.0)
                else:
                    tile = tile - level_ridge * weights[h]
                table[h].append(tile)
        solved = solve(table, blocks)
        return tuple(
            weights[h] + jnp.broadcast_to(solved[h][0:1], (SUBLANES, LANES))
            for h in range(RIDGES)
        )

    start = tuple(jnp.zeros((SUBLANES, LANES), jnp.float32) for _ in range(RIDGES))
    weights = lax.fori_loop(0, NEWTON, step, start)
    out[...] = jnp.concatenate([w[0:1] for w in weights], axis=0)


def newton(arrived, target, blocks):
    rows, samples = arrived.shape
    traits = target.shape[0]
    predictors = rows // traits
    weights = pl.pallas_call(
        functools.partial(newton_kernel, traits, blocks),
        out_shape=jax.ShapeDtypeStruct((RIDGES, LANES), jnp.float32),
        in_specs=[pl.BlockSpec(memory_space=pltpu.VMEM)] * 2,
        out_specs=pl.BlockSpec(memory_space=pltpu.VMEM),
        scratch_shapes=[
            pltpu.VMEM((rows, samples), jnp.bfloat16),
            pltpu.VMEM((traits // 2, 2 * predictors + 2 * traits, samples), jnp.bfloat16),
        ],
        compiler_params=pltpu.CompilerParams(vmem_limit_bytes=48 << 20),
        name="newton",
    )(arrived, target)
    return weights.reshape(RIDGES, traits, blocks).swapaxes(0, 1).reshape(traits, predictors)


def fit_traits(arrived, target):
    rows, samples = arrived.shape
    count = target.shape[0]
    predictors = rows // count
    design = arrived.reshape(-1, RIDGES, count, samples).transpose(2, 0, 1, 3)
    design = design.reshape(count, predictors, samples)
    level_ridge = LEVEL_ONE * samples
    weights = jnp.zeros((count, predictors), jnp.float32)
    identity = jnp.eye(predictors, dtype=jnp.float32)
    for _ in range(NEWTON):
        logits = jnp.einsum(
            "kqn,kq->kn", design, weights.astype(jnp.bfloat16), preferred_element_type=jnp.float32
        )
        prob = jax.nn.sigmoid(logits)
        resid = (target - prob).astype(jnp.bfloat16)
        weighted = (design * (prob * (1.0 - prob))[:, None, :]).astype(jnp.bfloat16)
        gram = jnp.einsum("kqn,kpn->kqp", weighted, design, preferred_element_type=jnp.float32)
        grad = jnp.einsum("kqn,kn->kq", design, resid, preferred_element_type=jnp.float32)
        grad = grad - level_ridge * weights
        factor = jnp.linalg.cholesky(gram + level_ridge * identity)
        partial_solve = lax.linalg.triangular_solve(
            factor, grad[:, :, None], left_side=True, lower=True
        )
        update = lax.linalg.triangular_solve(
            factor, partial_solve, left_side=True, lower=True, transpose_a=True
        )
        weights = weights + update[:, :, 0]
    return weights.reshape(count, -1, RIDGES).swapaxes(1, 2).reshape(count, predictors)


def on_device(dosage, eigvec, eigval, pheno):
    samples, width = dosage.shape
    traits = pheno.shape[1]
    regions = lax.axis_size("region")
    per_device = traits // regions
    shrink = jnp.array([width * (1.0 - value) / value for value in HERITABILITY], jnp.float32)
    std_trait = standardize(pheno)
    std_geno = standardize(dosage)
    cross = lax.dot_general(
        std_trait, std_geno, (((0,), (0,)), ((), ())), preferred_element_type=jnp.float32
    ).astype(jnp.bfloat16)
    rotated = jnp.dot(cross, eigvec, preferred_element_type=jnp.float32)
    scaled = rotated.reshape(regions, 1, per_device, width) / (
        eigval[0][None, None, None, :] + shrink[None, :, None, None]
    )
    scaled = scaled.astype(jnp.bfloat16).reshape(RIDGES * traits, width)
    ridge = lax.dot_general(
        scaled, eigvec, (((1,), (1,)), ((), ())), preferred_element_type=jnp.float32
    ).astype(jnp.bfloat16)
    predicted = lax.dot_general(
        ridge, std_geno, (((1,), (1,)), ((), ())), preferred_element_type=jnp.float32
    ).astype(jnp.bfloat16)
    arrived = lax.all_to_all(predicted, "region", split_axis=0, concat_axis=0, tiled=True)
    position = lax.axis_index("region")
    target = lax.dynamic_slice_in_dim(pheno, position * per_device, per_device, 1)
    target = target.astype(jnp.float32).T
    if per_device == SUBLANES and per_device * regions == LANES:
        return newton(arrived, target, regions)
    return fit_traits(arrived, target)


def solution(mesh):
    return jax.shard_map(
        on_device,
        mesh=mesh,
        in_specs=(
            P("cohort", "region"),
            P("region", "cohort"),
            P("cohort", "region"),
            P("cohort", None),
        ),
        out_specs=P("region", "cohort"),
        check_vma=False,
    )
```

```python
import functools

import jax
import jax.numpy as jnp
from jax import lax
from jax.experimental import pallas as pl
from jax.experimental.pallas import tpu as pltpu
from jax.sharding import PartitionSpec as P

NEWTON = 3
EPSILON = 1e-05
HERITABILITY = (0.01, 0.25, 0.75, 0.99)
LEVEL_ONE = 0.03125
RIDGES = len(HERITABILITY)
LANES = 128
SUBLANES = 8
TILE = 256
WIDE = 512


def level_zero_kernel(
    dosage_hbm, eigvec_hbm, eigval, pheno, out_hbm, dosage, eigvec, covariance, squares, scaled, slope, predicted, sems
):
    samples, width = dosage.shape
    traits = pheno.shape[1]
    chunks = width // TILE
    copies = [
        pltpu.make_async_copy(
            dosage_hbm.at[:, pl.ds(c * TILE, TILE)], dosage.at[:, pl.ds(c * TILE, TILE)], sems.at[c]
        )
        for c in range(chunks)
    ]
    basis = pltpu.make_async_copy(eigvec_hbm, eigvec, sems.at[chunks])
    for copy in copies:
        copy.start()
    basis.start()

    row = lax.broadcasted_iota(jnp.int32, (traits, traits), 0)
    column = lax.broadcasted_iota(jnp.int32, (traits, traits), 1)
    turned = lax.dot_general(
        jnp.where(row == column, 1.0, 0.0).astype(jnp.bfloat16),
        pheno[...],
        (((1,), (1,)), ((), ())),
        preferred_element_type=jnp.float32,
    )
    cases = jnp.sum(turned, axis=1, keepdims=True)
    center = cases / samples
    spread = jnp.sqrt(
        (cases * samples - cases * cases) / (samples * float(samples)) + EPSILON
    )
    ones = ((1.0 - center) / spread).astype(jnp.bfloat16).astype(jnp.float32)
    zeros = ((0.0 - center) / spread).astype(jnp.bfloat16).astype(jnp.float32)
    delta = ones - zeros
    left = jnp.concatenate([turned, jnp.ones((2 * SUBLANES, samples), jnp.float32)], axis=0).astype(
        jnp.bfloat16
    )
    for c in range(chunks):
        copies[c].wait()
        part = dosage[:, c * TILE : (c + 1) * TILE]
        covariance[:, c * TILE : (c + 1) * TILE] = jnp.dot(
            left, part, preferred_element_type=jnp.float32
        )
        square = part * part
        rows = samples
        while rows > 4 * SUBLANES:
            rows //= 2
            square = square[:rows] + square[rows : 2 * rows]
        squares[:, c * TILE : (c + 1) * TILE] = jnp.sum(
            square.astype(jnp.float32), axis=0, keepdims=True
        )
    total = covariance[traits : traits + 1, :]
    mean = total / samples
    deviation = jnp.sqrt(
        (squares[...] * samples - total * total) / (samples * float(samples)) + EPSILON
    )
    inverse = 1.0 / deviation
    cross = (
        (covariance[:traits, :] - cases * mean) * delta * inverse
    ).astype(jnp.bfloat16)
    basis.wait()
    rotated = jnp.dot(cross, eigvec[...], preferred_element_type=jnp.float32)
    for r, value in enumerate(HERITABILITY):
        shrunk = rotated * (1.0 / (eigval[...] + width * (1.0 - value) / value))
        for g in range(traits // SUBLANES):
            start = (g * RIDGES + r) * SUBLANES
            scaled[start : start + SUBLANES, :] = shrunk[
                g * SUBLANES : (g + 1) * SUBLANES
            ].astype(jnp.bfloat16)
    for c in range(chunks):
        ridge = lax.dot_general(
            scaled[...],
            eigvec[c * TILE : (c + 1) * TILE, :],
            (((1,), (1,)), ((), ())),
            preferred_element_type=jnp.float32,
        )
        slope[:, c * TILE : (c + 1) * TILE] = (
            ridge * inverse[:, c * TILE : (c + 1) * TILE]
        ).astype(jnp.bfloat16)
    high = mean.astype(jnp.bfloat16).astype(jnp.float32)
    low = (mean - high).astype(jnp.bfloat16).astype(jnp.float32)
    rest = mean - high - low
    place = lax.broadcasted_iota(jnp.int32, (2 * SUBLANES, width), 0)
    means = jnp.where(place == 0, high, jnp.where(place == 1, low, jnp.where(place == 2, rest, 0.0)))
    offset = jnp.sum(
        lax.dot_general(
            slope[...],
            means.astype(jnp.bfloat16),
            (((1,), (1,)), ((), ())),
            preferred_element_type=jnp.float32,
        ),
        axis=1,
        keepdims=True,
    )
    outs = []
    for n in range(samples // WIDE):
        found = lax.dot_general(
            slope[...],
            dosage[n * WIDE : (n + 1) * WIDE, :],
            (((1,), (1,)), ((), ())),
            preferred_element_type=jnp.float32,
        )
        predicted[:, n * WIDE : (n + 1) * WIDE] = (found - offset).astype(jnp.bfloat16)
        copy = pltpu.make_async_copy(
            predicted.at[:, pl.ds(n * WIDE, WIDE)],
            out_hbm.at[:, pl.ds(n * WIDE, WIDE)],
            sems.at[chunks + 1 + n],
        )
        copy.start()
        outs.append(copy)
    for copy in outs:
        copy.wait()


def level_zero(dosage, eigvec, eigval, pheno):
    samples, width = dosage.shape
    traits = pheno.shape[1]
    rows = RIDGES * traits
    anywhere = pl.BlockSpec(memory_space=pl.ANY)
    inside = pl.BlockSpec(memory_space=pltpu.VMEM)
    return pl.pallas_call(
        level_zero_kernel,
        out_shape=jax.ShapeDtypeStruct((rows, samples), jnp.bfloat16),
        in_specs=[anywhere, anywhere, inside, inside],
        out_specs=anywhere,
        scratch_shapes=[
            pltpu.VMEM((samples, width), jnp.bfloat16),
            pltpu.VMEM((width, width), jnp.bfloat16),
            pltpu.VMEM((traits + 2 * SUBLANES, width), jnp.float32),
            pltpu.VMEM((1, width), jnp.float32),
            pltpu.VMEM((rows, width), jnp.bfloat16),
            pltpu.VMEM((rows, width), jnp.bfloat16),
            pltpu.VMEM((rows, samples), jnp.bfloat16),
            pltpu.SemaphoreType.DMA((width // TILE + 1 + samples // WIDE,)),
        ],
        compiler_params=pltpu.CompilerParams(vmem_limit_bytes=48 << 20),
        name="level_zero",
    )(dosage, eigvec, eigval, pheno)


def reorder_matrix(traits, blocks, parts):
    size = blocks * RIDGES * traits // parts
    row = lax.broadcasted_iota(jnp.int32, (size, size), 0)
    column = lax.broadcasted_iota(jnp.int32, (size, size), 1)
    group = blocks // parts
    block, rest = row % group, row // group
    ridge, pair = rest % RIDGES, rest // RIDGES
    trait = (pair % 2) * (traits // 2) + pair // 2
    return jnp.where(column == (block * RIDGES + ridge) * traits + trait, 1.0, 0.0).astype(
        jnp.bfloat16
    )


def inverse_two(m):
    (a, b), (c, d) = m
    scale = 1.0 / (a * d - b * c)
    return ((d * scale, -b * scale), (-c * scale, a * scale))


def product(x, y):
    return tuple(
        tuple(x[i][0] * y[0][j] + x[i][1] * y[1][j] for j in range(2)) for i in range(2)
    )


def negative(x):
    return tuple(tuple(-value for value in row) for row in x)


def inverse_four(m):
    def corner(i, j):
        return ((m[i][j], m[i][j + 1]), (m[i + 1][j], m[i + 1][j + 1]))

    first = inverse_two(corner(0, 0))
    left = product(corner(2, 0), first)
    right = product(first, corner(0, 2))
    inner = product(left, corner(0, 2))
    last = corner(2, 2)
    second = inverse_two(
        tuple(tuple(last[i][j] - inner[i][j] for j in range(2)) for i in range(2))
    )
    below = product(second, left)
    back = product(right, below)
    top = tuple(tuple(first[i][j] + back[i][j] for j in range(2)) for i in range(2))
    beside, below = negative(product(right, second)), negative(below)
    return [list(top[i]) + list(beside[i]) for i in range(2)] + [
        list(below[i]) + list(second[i]) for i in range(2)
    ]


def gather_lanes(tile, lanes):
    return jnp.take_along_axis(tile, lanes, axis=1)


def solve(table, span):
    heights, tiles = len(table), len(table[0])
    lane = lax.broadcasted_iota(jnp.int32, (SUBLANES, LANES), 1)
    within = lane % span
    for k in range(0, (tiles - 1) * SUBLANES, 4):
        home, low = k // span, k % span
        first, sub = k // SUBLANES, k % SUBLANES
        rows = [
            [gather_lanes(table[home][r], (lane - within) + low + m) for r in range(first, tiles)]
            for m in range(4)
        ]
        columns = [
            [
                jnp.broadcast_to(table[h][first][sub + m : sub + m + 1], (SUBLANES, LANES))
                for h in range(heights)
            ]
            for m in range(4)
        ]
        pivot = [
            [
                jnp.broadcast_to(rows[m][0][sub + n : sub + n + 1], (SUBLANES, LANES))
                for n in range(4)
            ]
            for m in range(4)
        ]
        inverse = inverse_four(pivot)
        chosen = (within >= low) & (within < low + 4)
        for h in range(heights):
            factors = []
            for n in range(4):
                factor = (columns[0][h] * inverse[0][n] + columns[1][h] * inverse[1][n]) + (
                    columns[2][h] * inverse[2][n] + columns[3][h] * inverse[3][n]
                )
                if h == home:
                    for m in range(4):
                        factor = jnp.where(within == low + m, -inverse[m][n], factor)
                factors.append(factor)
            for r in range(first, tiles):
                base = table[h][r]
                if h == home:
                    base = jnp.where(chosen, 0.0, base)
                table[h][r] = (
                    base
                    - (factors[0] * rows[0][r - first] + factors[1] * rows[1][r - first])
                    - (factors[2] * rows[2][r - first] + factors[3] * rows[3][r - first])
                )
    return [table[h][tiles - 1] for h in range(heights)]


def exchange(tiles, span):
    lane = lax.broadcasted_iota(jnp.int32, (SUBLANES, LANES), 1)
    tiles = list(tiles)
    for bit in (1, 2):
        shift = bit * span
        odd = (lane // shift) % 2 == 1
        for i in range(4):
            if not i & bit:
                x, y = tiles[i], tiles[i | bit]
                tiles[i] = jnp.where(odd, pltpu.roll(y, shift, 1), x)
                tiles[i | bit] = jnp.where(odd, y, pltpu.roll(x, LANES - shift, 1))
    return tiles


def newton_kernel(traits, blocks, arrived, target, out, design, lhs):
    samples = arrived.shape[1]
    predictors = RIDGES * blocks
    half = traits // 2
    parts = arrived.shape[0] // TILE
    order = reorder_matrix(traits, blocks, parts)
    group = blocks // parts
    for part in range(parts):
        moved = jnp.dot(
            order, arrived[part * TILE : (part + 1) * TILE, :], preferred_element_type=jnp.float32
        )
        for i in range(TILE // group):
            start = i * blocks + part * group
            design[start : start + group, :] = moved[i * group : (i + 1) * group].astype(
                jnp.bfloat16
            )
    level_ridge = LEVEL_ONE * samples
    lane = lax.broadcasted_iota(jnp.int32, (SUBLANES, LANES), 1)
    sub = lax.broadcasted_iota(jnp.int32, (SUBLANES, LANES), 0)
    upper = lane >= predictors
    pheno = target[...]
    middle = predictors + 2 * traits

    def step(_, weights):
        spread_out = [
            jnp.where((lane // predictors) * half + s == sub, w, 0.0).astype(jnp.bfloat16)
            for s, w in enumerate(exchange(weights, blocks))
        ]
        logits = jnp.dot(
            jnp.concatenate(spread_out, axis=1), design[...], preferred_element_type=jnp.float32
        )
        prob = 1.0 / (1.0 + jnp.exp(-logits))
        curve = prob * (1.0 - prob)
        resid = pheno - prob
        resid = jnp.concatenate([resid, jnp.zeros_like(resid)], axis=0).astype(jnp.bfloat16)
        found = []
        for s in range(half):
            base = s * 2 * predictors
            for start, trait, place in ((0, s, 0), (predictors, s + half, middle)):
                own = design[base + start : base + start + predictors, :].astype(jnp.float32)
                lhs[s, place : place + predictors, :] = (own * curve[trait : trait + 1, :]).astype(
                    jnp.bfloat16
                )
            lhs[s, predictors:middle, :] = resid
            result = lax.dot_general(
                lhs[s],
                design[base : base + 2 * predictors, :],
                (((1,), (1,)), ((), ())),
                preferred_element_type=jnp.float32,
            )
            tiles = [
                jnp.where(
                    upper,
                    result[middle + SUBLANES * r : middle + SUBLANES * (r + 1)],
                    result[SUBLANES * r : SUBLANES * (r + 1)],
                )
                for r in range(predictors // SUBLANES)
            ]
            first, second = predictors + s, predictors + s + half
            tiles.append(
                jnp.where(
                    upper[:1], result[second : second + 1], result[first : first + 1]
                )
                + jnp.zeros((SUBLANES, LANES), jnp.float32)
            )
            found.append(tiles)
        table = [[] for _ in range(RIDGES)]
        for r in range(predictors // SUBLANES + 1):
            for h, tile in enumerate(exchange([found[s][r] for s in range(half)], blocks)):
                if r < predictors // SUBLANES:
                    same = SUBLANES * r + sub == h * blocks + lane % blocks
                    tile = tile + jnp.where(same, level_ridge, 0.0)
                else:
                    tile = tile - level_ridge * weights[h]
                table[h].append(tile)
        solved = solve(table, blocks)
        return tuple(
            weights[h] + jnp.broadcast_to(solved[h][0:1], (SUBLANES, LANES))
            for h in range(RIDGES)
        )

    start = tuple(jnp.zeros((SUBLANES, LANES), jnp.float32) for _ in range(RIDGES))
    weights = lax.fori_loop(0, NEWTON, step, start)
    out[...] = jnp.concatenate([w[0:1] for w in weights], axis=0)


def newton(arrived, target, blocks):
    rows, samples = arrived.shape
    traits = target.shape[0]
    predictors = rows // traits
    weights = pl.pallas_call(
        functools.partial(newton_kernel, traits, blocks),
        out_shape=jax.ShapeDtypeStruct((RIDGES, LANES), jnp.float32),
        in_specs=[pl.BlockSpec(memory_space=pltpu.VMEM)] * 2,
        out_specs=pl.BlockSpec(memory_space=pltpu.VMEM),
        scratch_shapes=[
            pltpu.VMEM((rows, samples), jnp.bfloat16),
            pltpu.VMEM((traits // 2, 2 * predictors + 2 * traits, samples), jnp.bfloat16),
        ],
        compiler_params=pltpu.CompilerParams(vmem_limit_bytes=48 << 20),
        name="newton",
    )(arrived, target)
    return weights.reshape(RIDGES, traits, blocks).swapaxes(0, 1).reshape(traits, predictors)


def fit_traits(arrived, target):
    rows, samples = arrived.shape
    count = target.shape[0]
    predictors = rows // count
    design = arrived.reshape(-1, RIDGES, count, samples).transpose(2, 0, 1, 3)
    design = design.reshape(count, predictors, samples)
    level_ridge = LEVEL_ONE * samples
    weights = jnp.zeros((count, predictors), jnp.float32)
    identity = jnp.eye(predictors, dtype=jnp.float32)
    for _ in range(NEWTON):
        logits = jnp.einsum(
            "kqn,kq->kn", design, weights.astype(jnp.bfloat16), preferred_element_type=jnp.float32
        )
        prob = jax.nn.sigmoid(logits)
        resid = (target - prob).astype(jnp.bfloat16)
        weighted = (design * (prob * (1.0 - prob))[:, None, :]).astype(jnp.bfloat16)
        gram = jnp.einsum("kqn,kpn->kqp", weighted, design, preferred_element_type=jnp.float32)
        grad = jnp.einsum("kqn,kn->kq", design, resid, preferred_element_type=jnp.float32)
        grad = grad - level_ridge * weights
        factor = jnp.linalg.cholesky(gram + level_ridge * identity)
        partial_solve = lax.linalg.triangular_solve(
            factor, grad[:, :, None], left_side=True, lower=True
        )
        update = lax.linalg.triangular_solve(
            factor, partial_solve, left_side=True, lower=True, transpose_a=True
        )
        weights = weights + update[:, :, 0]
    return weights.reshape(count, -1, RIDGES).swapaxes(1, 2).reshape(count, predictors)


def on_device(dosage, eigvec, eigval, pheno):
    traits = pheno.shape[1]
    regions = lax.axis_size("region")
    per_device = traits // regions
    predicted = level_zero(dosage, eigvec, eigval, pheno)
    if per_device != SUBLANES:
        predicted = predicted.reshape(-1, RIDGES, SUBLANES // per_device, per_device, dosage.shape[0])
        predicted = predicted.swapaxes(1, 2).reshape(RIDGES * traits, dosage.shape[0])
    arrived = lax.all_to_all(predicted, "region", split_axis=0, concat_axis=0, tiled=True)
    position = lax.axis_index("region")
    target = lax.dynamic_slice_in_dim(pheno, position * per_device, per_device, 1)
    target = target.astype(jnp.float32).T
    if per_device == SUBLANES and per_device * regions == LANES:
        return newton(arrived, target, regions)
    return fit_traits(arrived, target)


def solution(mesh):
    return jax.shard_map(
        on_device,
        mesh=mesh,
        in_specs=(
            P("cohort", "region"),
            P("region", "cohort"),
            P("cohort", "region"),
            P("cohort", None),
        ),
        out_specs=P("region", "cohort"),
        check_vma=False,
    )
```

```python
import functools

import jax
import jax.numpy as jnp
from jax import lax
from jax.experimental import pallas as pl
from jax.experimental.pallas import tpu as pltpu
from jax.sharding import PartitionSpec as P

NEWTON = 3
EPSILON = 1e-05
HERITABILITY = (0.01, 0.25, 0.75, 0.99)
LEVEL_ONE = 0.03125
RIDGES = len(HERITABILITY)
LANES = 128
SUBLANES = 8
TILE = 256
WIDE = 512


def level_zero_kernel(
    dosage_hbm,
    eigvec_hbm,
    eigval_hbm,
    pheno_hbm,
    out_hbm,
    dosage,
    eigvec,
    eigval,
    pheno,
    covariance,
    squares,
    scaled,
    slope,
    predicted,
    sems,
):
    samples, width = dosage.shape
    traits = pheno.shape[1]
    chunks = width // TILE
    copies = [
        pltpu.make_async_copy(
            dosage_hbm.at[:, pl.ds(c * TILE, TILE)], dosage.at[:, pl.ds(c * TILE, TILE)], sems.at[c]
        )
        for c in range(chunks)
    ]
    cases_copy = pltpu.make_async_copy(pheno_hbm, pheno, sems.at[chunks])
    basis = pltpu.make_async_copy(eigvec_hbm, eigvec, sems.at[chunks + 1])
    values = pltpu.make_async_copy(eigval_hbm, eigval, sems.at[chunks + 2])
    cases_copy.start()
    for copy in copies:
        copy.start()
    basis.start()
    values.start()

    row = lax.broadcasted_iota(jnp.int32, (traits, traits), 0)
    column = lax.broadcasted_iota(jnp.int32, (traits, traits), 1)
    cases_copy.wait()
    turned = lax.dot_general(
        jnp.where(row == column, 1.0, 0.0).astype(jnp.bfloat16),
        pheno[...],
        (((1,), (1,)), ((), ())),
        preferred_element_type=jnp.float32,
    )
    cases = jnp.sum(turned, axis=1, keepdims=True)
    center = cases / samples
    spread = jnp.sqrt(
        (cases * samples - cases * cases) / (samples * float(samples)) + EPSILON
    )
    ones = ((1.0 - center) / spread).astype(jnp.bfloat16).astype(jnp.float32)
    zeros = ((0.0 - center) / spread).astype(jnp.bfloat16).astype(jnp.float32)
    delta = ones - zeros
    left = jnp.concatenate([turned, jnp.ones((2 * SUBLANES, samples), jnp.float32)], axis=0).astype(
        jnp.bfloat16
    )
    for c in range(chunks):
        copies[c].wait()
        part = dosage[:, c * TILE : (c + 1) * TILE]
        covariance[:, c * TILE : (c + 1) * TILE] = jnp.dot(
            left, part, preferred_element_type=jnp.float32
        )
        square = part * part
        rows = samples
        while rows > 4 * SUBLANES:
            rows //= 2
            square = square[:rows] + square[rows : 2 * rows]
        squares[:, c * TILE : (c + 1) * TILE] = jnp.sum(
            square.astype(jnp.float32), axis=0, keepdims=True
        )
    total = covariance[traits : traits + 1, :]
    mean = total / samples
    deviation = jnp.sqrt(
        (squares[...] * samples - total * total) / (samples * float(samples)) + EPSILON
    )
    inverse = 1.0 / deviation
    cross = (
        (covariance[:traits, :] - cases * mean) * delta * inverse
    ).astype(jnp.bfloat16)
    basis.wait()
    values.wait()
    rotated = jnp.dot(cross, eigvec[...], preferred_element_type=jnp.float32)
    for r, value in enumerate(HERITABILITY):
        shrunk = rotated * (1.0 / (eigval[...] + width * (1.0 - value) / value))
        for g in range(traits // SUBLANES):
            start = (g * RIDGES + r) * SUBLANES
            scaled[start : start + SUBLANES, :] = shrunk[
                g * SUBLANES : (g + 1) * SUBLANES
            ].astype(jnp.bfloat16)
    for c in range(chunks):
        ridge = lax.dot_general(
            scaled[...],
            eigvec[c * TILE : (c + 1) * TILE, :],
            (((1,), (1,)), ((), ())),
            preferred_element_type=jnp.float32,
        )
        slope[:, c * TILE : (c + 1) * TILE] = (
            ridge * inverse[:, c * TILE : (c + 1) * TILE]
        ).astype(jnp.bfloat16)
    high = mean.astype(jnp.bfloat16).astype(jnp.float32)
    low = (mean - high).astype(jnp.bfloat16).astype(jnp.float32)
    rest = mean - high - low
    place = lax.broadcasted_iota(jnp.int32, (2 * SUBLANES, width), 0)
    means = jnp.where(place == 0, high, jnp.where(place == 1, low, jnp.where(place == 2, rest, 0.0)))
    offset = jnp.sum(
        lax.dot_general(
            slope[...],
            means.astype(jnp.bfloat16),
            (((1,), (1,)), ((), ())),
            preferred_element_type=jnp.float32,
        ),
        axis=1,
        keepdims=True,
    )
    outs = []
    for n in range(samples // WIDE):
        found = lax.dot_general(
            slope[...],
            dosage[n * WIDE : (n + 1) * WIDE, :],
            (((1,), (1,)), ((), ())),
            preferred_element_type=jnp.float32,
        )
        predicted[:, n * WIDE : (n + 1) * WIDE] = (found - offset).astype(jnp.bfloat16)
        copy = pltpu.make_async_copy(
            predicted.at[:, pl.ds(n * WIDE, WIDE)],
            out_hbm.at[:, pl.ds(n * WIDE, WIDE)],
            sems.at[chunks + 3 + n],
        )
        copy.start()
        outs.append(copy)
    for copy in outs:
        copy.wait()


def level_zero(dosage, eigvec, eigval, pheno):
    samples, width = dosage.shape
    traits = pheno.shape[1]
    rows = RIDGES * traits
    anywhere = pl.BlockSpec(memory_space=pl.ANY)
    return pl.pallas_call(
        level_zero_kernel,
        out_shape=jax.ShapeDtypeStruct((rows, samples), jnp.bfloat16),
        in_specs=[anywhere] * 4,
        out_specs=anywhere,
        scratch_shapes=[
            pltpu.VMEM((samples, width), jnp.bfloat16),
            pltpu.VMEM((width, width), jnp.bfloat16),
            pltpu.VMEM((1, width), jnp.float32),
            pltpu.VMEM((samples, traits), jnp.bfloat16),
            pltpu.VMEM((traits + 2 * SUBLANES, width), jnp.float32),
            pltpu.VMEM((1, width), jnp.float32),
            pltpu.VMEM((rows, width), jnp.bfloat16),
            pltpu.VMEM((rows, width), jnp.bfloat16),
            pltpu.VMEM((rows, samples), jnp.bfloat16),
            pltpu.SemaphoreType.DMA((width // TILE + 3 + samples // WIDE,)),
        ],
        compiler_params=pltpu.CompilerParams(vmem_limit_bytes=63 << 20),
        name="level_zero",
    )(dosage, eigvec, eigval, pheno)


def reorder_matrix(traits, blocks, parts):
    size = blocks * RIDGES * traits // parts
    row = lax.broadcasted_iota(jnp.int32, (size, size), 0)
    column = lax.broadcasted_iota(jnp.int32, (size, size), 1)
    group = blocks // parts
    block, rest = row % group, row // group
    ridge, pair = rest % RIDGES, rest // RIDGES
    trait = (pair % 2) * (traits // 2) + pair // 2
    return jnp.where(column == (block * RIDGES + ridge) * traits + trait, 1.0, 0.0).astype(
        jnp.bfloat16
    )


def inverse_two(m):
    (a, b), (c, d) = m
    scale = 1.0 / (a * d - b * c)
    return ((d * scale, -b * scale), (-c * scale, a * scale))


def product(x, y):
    return tuple(
        tuple(x[i][0] * y[0][j] + x[i][1] * y[1][j] for j in range(2)) for i in range(2)
    )


def negative(x):
    return tuple(tuple(-value for value in row) for row in x)


def inverse_four(m):
    def corner(i, j):
        return ((m[i][j], m[i][j + 1]), (m[i + 1][j], m[i + 1][j + 1]))

    first = inverse_two(corner(0, 0))
    left = product(corner(2, 0), first)
    right = product(first, corner(0, 2))
    inner = product(left, corner(0, 2))
    last = corner(2, 2)
    second = inverse_two(
        tuple(tuple(last[i][j] - inner[i][j] for j in range(2)) for i in range(2))
    )
    below = product(second, left)
    back = product(right, below)
    top = tuple(tuple(first[i][j] + back[i][j] for j in range(2)) for i in range(2))
    beside, below = negative(product(right, second)), negative(below)
    return [list(top[i]) + list(beside[i]) for i in range(2)] + [
        list(below[i]) + list(second[i]) for i in range(2)
    ]


def gather_lanes(tile, lanes):
    return jnp.take_along_axis(tile, lanes, axis=1)


def solve(table, span):
    heights, tiles = len(table), len(table[0])
    size = (tiles - 1) * SUBLANES
    lane = lax.broadcasted_iota(jnp.int32, (SUBLANES, LANES), 1)
    within = lane % span

    def pivot_rows(k):
        lanes = (lane - within) + k % span
        return [
            [gather_lanes(table[k // span][r], lanes + m) for r in range(k // SUBLANES, tiles)]
            for m in range(4)
        ]

    rows = pivot_rows(0)
    for k in range(0, size, 4):
        home, low = k // span, k % span
        first, sub = k // SUBLANES, k % SUBLANES
        pivot = [
            [
                jnp.broadcast_to(rows[m][0][sub + n : sub + n + 1], (SUBLANES, LANES))
                for n in range(4)
            ]
            for m in range(4)
        ]
        inverse = inverse_four(pivot)
        chosen = (within >= low) & (within < low + 4)
        after = min(k + 4, size - 4)
        current = rows
        for h in sorted(range(heights), key=lambda h: h != after // span):
            columns = [
                jnp.broadcast_to(table[h][first][sub + m : sub + m + 1], (SUBLANES, LANES))
                for m in range(4)
            ]
            factors = []
            for n in range(4):
                factor = (columns[0] * inverse[0][n] + columns[1] * inverse[1][n]) + (
                    columns[2] * inverse[2][n] + columns[3] * inverse[3][n]
                )
                if h == home:
                    for m in range(4):
                        factor = jnp.where(within == low + m, -inverse[m][n], factor)
                factors.append(factor)
            for r in range(first, tiles):
                base = table[h][r]
                if h == home:
                    base = jnp.where(chosen, 0.0, base)
                values = [current[m][r - first] for m in range(4)]
                table[h][r] = (
                    base
                    - (factors[0] * values[0] + factors[1] * values[1])
                    - (factors[2] * values[2] + factors[3] * values[3])
                )
            if h == after // span and k < after:
                rows = pivot_rows(after)
    return [table[h][tiles - 1] for h in range(heights)]


def exchange(tiles, span):
    lane = lax.broadcasted_iota(jnp.int32, (SUBLANES, LANES), 1)
    tiles = list(tiles)
    for bit in (1, 2):
        shift = bit * span
        odd = (lane // shift) % 2 == 1
        for i in range(4):
            if not i & bit:
                x, y = tiles[i], tiles[i | bit]
                tiles[i] = jnp.where(odd, pltpu.roll(y, shift, 1), x)
                tiles[i | bit] = jnp.where(odd, y, pltpu.roll(x, LANES - shift, 1))
    return tiles


def newton_kernel(traits, blocks, arrived, target, out, design, lhs):
    samples = arrived.shape[1]
    predictors = RIDGES * blocks
    half = traits // 2
    parts = arrived.shape[0] // TILE
    order = reorder_matrix(traits, blocks, parts)
    group = blocks // parts
    for part in range(parts):
        moved = jnp.dot(
            order, arrived[part * TILE : (part + 1) * TILE, :], preferred_element_type=jnp.float32
        )
        for i in range(TILE // group):
            start = i * blocks + part * group
            design[start : start + group, :] = moved[i * group : (i + 1) * group].astype(
                jnp.bfloat16
            )
    level_ridge = LEVEL_ONE * samples
    lane = lax.broadcasted_iota(jnp.int32, (SUBLANES, LANES), 1)
    sub = lax.broadcasted_iota(jnp.int32, (SUBLANES, LANES), 0)
    upper = lane >= predictors
    pheno = target[...]
    middle = predictors + 2 * traits

    def step(_, weights):
        spread_out = [
            jnp.where((lane // predictors) * half + s == sub, w, 0.0).astype(jnp.bfloat16)
            for s, w in enumerate(exchange(weights, blocks))
        ]
        logits = jnp.dot(
            jnp.concatenate(spread_out, axis=1), design[...], preferred_element_type=jnp.float32
        )
        prob = 1.0 / (1.0 + jnp.exp(-logits))
        curve = prob * (1.0 - prob)
        resid = pheno - prob
        resid = jnp.concatenate([resid, jnp.zeros_like(resid)], axis=0).astype(jnp.bfloat16)
        found = []
        for s in range(half):
            base = s * 2 * predictors
            for start, trait, place in ((0, s, 0), (predictors, s + half, middle)):
                own = design[base + start : base + start + predictors, :].astype(jnp.float32)
                lhs[s, place : place + predictors, :] = (own * curve[trait : trait + 1, :]).astype(
                    jnp.bfloat16
                )
            lhs[s, predictors:middle, :] = resid
            result = lax.dot_general(
                lhs[s],
                design[base : base + 2 * predictors, :],
                (((1,), (1,)), ((), ())),
                preferred_element_type=jnp.float32,
            )
            tiles = [
                jnp.where(
                    upper,
                    result[middle + SUBLANES * r : middle + SUBLANES * (r + 1)],
                    result[SUBLANES * r : SUBLANES * (r + 1)],
                )
                for r in range(predictors // SUBLANES)
            ]
            first, second = predictors + s, predictors + s + half
            tiles.append(
                jnp.where(
                    upper[:1], result[second : second + 1], result[first : first + 1]
                )
                + jnp.zeros((SUBLANES, LANES), jnp.float32)
            )
            found.append(tiles)
        table = [[] for _ in range(RIDGES)]
        for r in range(predictors // SUBLANES + 1):
            for h, tile in enumerate(exchange([found[s][r] for s in range(half)], blocks)):
                if r < predictors // SUBLANES:
                    same = SUBLANES * r + sub == h * blocks + lane % blocks
                    tile = tile + jnp.where(same, level_ridge, 0.0)
                else:
                    tile = tile - level_ridge * weights[h]
                table[h].append(tile)
        solved = solve(table, blocks)
        return tuple(
            weights[h] + jnp.broadcast_to(solved[h][0:1], (SUBLANES, LANES))
            for h in range(RIDGES)
        )

    start = tuple(jnp.zeros((SUBLANES, LANES), jnp.float32) for _ in range(RIDGES))
    weights = lax.fori_loop(0, NEWTON, step, start)
    out[...] = jnp.concatenate([w[0:1] for w in weights], axis=0)


def newton(arrived, target, blocks):
    rows, samples = arrived.shape
    traits = target.shape[0]
    predictors = rows // traits
    weights = pl.pallas_call(
        functools.partial(newton_kernel, traits, blocks),
        out_shape=jax.ShapeDtypeStruct((RIDGES, LANES), jnp.float32),
        in_specs=[pl.BlockSpec(memory_space=pltpu.VMEM)] * 2,
        out_specs=pl.BlockSpec(memory_space=pltpu.VMEM),
        scratch_shapes=[
            pltpu.VMEM((rows, samples), jnp.bfloat16),
            pltpu.VMEM((traits // 2, 2 * predictors + 2 * traits, samples), jnp.bfloat16),
        ],
        compiler_params=pltpu.CompilerParams(vmem_limit_bytes=48 << 20),
        name="newton",
    )(arrived, target)
    return weights.reshape(RIDGES, traits, blocks).swapaxes(0, 1).reshape(traits, predictors)


def fit_traits(arrived, target):
    rows, samples = arrived.shape
    count = target.shape[0]
    predictors = rows // count
    design = arrived.reshape(-1, RIDGES, count, samples).transpose(2, 0, 1, 3)
    design = design.reshape(count, predictors, samples)
    level_ridge = LEVEL_ONE * samples
    weights = jnp.zeros((count, predictors), jnp.float32)
    identity = jnp.eye(predictors, dtype=jnp.float32)
    for _ in range(NEWTON):
        logits = jnp.einsum(
            "kqn,kq->kn", design, weights.astype(jnp.bfloat16), preferred_element_type=jnp.float32
        )
        prob = jax.nn.sigmoid(logits)
        resid = (target - prob).astype(jnp.bfloat16)
        weighted = (design * (prob * (1.0 - prob))[:, None, :]).astype(jnp.bfloat16)
        gram = jnp.einsum("kqn,kpn->kqp", weighted, design, preferred_element_type=jnp.float32)
        grad = jnp.einsum("kqn,kn->kq", design, resid, preferred_element_type=jnp.float32)
        grad = grad - level_ridge * weights
        factor = jnp.linalg.cholesky(gram + level_ridge * identity)
        partial_solve = lax.linalg.triangular_solve(
            factor, grad[:, :, None], left_side=True, lower=True
        )
        update = lax.linalg.triangular_solve(
            factor, partial_solve, left_side=True, lower=True, transpose_a=True
        )
        weights = weights + update[:, :, 0]
    return weights.reshape(count, -1, RIDGES).swapaxes(1, 2).reshape(count, predictors)


def on_device(dosage, eigvec, eigval, pheno):
    traits = pheno.shape[1]
    regions = lax.axis_size("region")
    per_device = traits // regions
    predicted = level_zero(dosage, eigvec, eigval, pheno)
    if per_device != SUBLANES:
        predicted = predicted.reshape(-1, RIDGES, SUBLANES // per_device, per_device, dosage.shape[0])
        predicted = predicted.swapaxes(1, 2).reshape(RIDGES * traits, dosage.shape[0])
    arrived = lax.all_to_all(predicted, "region", split_axis=0, concat_axis=0, tiled=True)
    position = lax.axis_index("region")
    target = lax.dynamic_slice_in_dim(pheno, position * per_device, per_device, 1)
    target = target.astype(jnp.float32).T
    if per_device == SUBLANES and per_device * regions == LANES:
        return newton(arrived, target, regions)
    return fit_traits(arrived, target)


def solution(mesh):
    return jax.shard_map(
        on_device,
        mesh=mesh,
        in_specs=(
            P("cohort", "region"),
            P("region", "cohort"),
            P("cohort", "region"),
            P("cohort", None),
        ),
        out_specs=P("region", "cohort"),
        check_vma=False,
    )
```

```python
import functools

import jax
import jax.numpy as jnp
from jax import lax
from jax.experimental import pallas as pl
from jax.experimental.pallas import tpu as pltpu
from jax.sharding import PartitionSpec as P

NEWTON = 3
EPSILON = 1e-05
HERITABILITY = (0.01, 0.25, 0.75, 0.99)
LEVEL_ONE = 0.03125
RIDGES = len(HERITABILITY)
LANES = 128
SUBLANES = 8
TILE = 256
WIDE = 512


def level_zero_kernel(
    dosage_hbm,
    eigvec_hbm,
    eigval_hbm,
    pheno_hbm,
    out_hbm,
    dosage,
    eigvec,
    eigval,
    pheno,
    covariance,
    squares,
    scaled,
    slope,
    predicted,
    sems,
):
    samples, width = dosage.shape
    traits = pheno.shape[1]
    chunks = width // TILE
    copies = [
        pltpu.make_async_copy(
            dosage_hbm.at[:, pl.ds(c * TILE, TILE)], dosage.at[:, pl.ds(c * TILE, TILE)], sems.at[c]
        )
        for c in range(chunks)
    ]
    cases_copy = pltpu.make_async_copy(pheno_hbm, pheno, sems.at[chunks])
    basis = pltpu.make_async_copy(eigvec_hbm, eigvec, sems.at[chunks + 1])
    values = pltpu.make_async_copy(eigval_hbm, eigval, sems.at[chunks + 2])
    cases_copy.start()
    for copy in copies:
        copy.start()
    basis.start()
    values.start()

    row = lax.broadcasted_iota(jnp.int32, (traits, traits), 0)
    column = lax.broadcasted_iota(jnp.int32, (traits, traits), 1)
    cases_copy.wait()
    turned = lax.dot_general(
        jnp.where(row == column, 1.0, 0.0).astype(jnp.bfloat16),
        pheno[...],
        (((1,), (1,)), ((), ())),
        preferred_element_type=jnp.float32,
    )
    cases = jnp.sum(turned, axis=1, keepdims=True)
    center = cases / samples
    spread = jnp.sqrt(
        (cases * samples - cases * cases) / (samples * float(samples)) + EPSILON
    )
    ones = ((1.0 - center) / spread).astype(jnp.bfloat16).astype(jnp.float32)
    zeros = ((0.0 - center) / spread).astype(jnp.bfloat16).astype(jnp.float32)
    delta = ones - zeros
    left = jnp.concatenate([turned, jnp.ones((2 * SUBLANES, samples), jnp.float32)], axis=0).astype(
        jnp.bfloat16
    )
    for c in range(chunks):
        copies[c].wait()
        part = dosage[:, c * TILE : (c + 1) * TILE]
        covariance[:, c * TILE : (c + 1) * TILE] = jnp.dot(
            left, part, preferred_element_type=jnp.float32
        )
        square = part * part
        rows = samples
        while rows > 4 * SUBLANES:
            rows //= 2
            square = square[:rows] + square[rows : 2 * rows]
        squares[:, c * TILE : (c + 1) * TILE] = jnp.sum(
            square.astype(jnp.float32), axis=0, keepdims=True
        )
    total = covariance[traits : traits + 1, :]
    mean = total / samples
    deviation = jnp.sqrt(
        (squares[...] * samples - total * total) / (samples * float(samples)) + EPSILON
    )
    inverse = 1.0 / deviation
    cross = (
        (covariance[:traits, :] - cases * mean) * delta * inverse
    ).astype(jnp.bfloat16)
    basis.wait()
    values.wait()
    rotated = jnp.dot(cross, eigvec[...], preferred_element_type=jnp.float32)
    for r, value in enumerate(HERITABILITY):
        shrunk = rotated * (1.0 / (eigval[...] + width * (1.0 - value) / value))
        for g in range(traits // SUBLANES):
            start = (g * RIDGES + r) * SUBLANES
            scaled[start : start + SUBLANES, :] = shrunk[
                g * SUBLANES : (g + 1) * SUBLANES
            ].astype(jnp.bfloat16)
    for c in range(chunks):
        ridge = lax.dot_general(
            scaled[...],
            eigvec[c * TILE : (c + 1) * TILE, :],
            (((1,), (1,)), ((), ())),
            preferred_element_type=jnp.float32,
        )
        slope[:, c * TILE : (c + 1) * TILE] = (
            ridge * inverse[:, c * TILE : (c + 1) * TILE]
        ).astype(jnp.bfloat16)
    high = mean.astype(jnp.bfloat16).astype(jnp.float32)
    low = (mean - high).astype(jnp.bfloat16).astype(jnp.float32)
    rest = mean - high - low
    place = lax.broadcasted_iota(jnp.int32, (2 * SUBLANES, width), 0)
    means = jnp.where(place == 0, high, jnp.where(place == 1, low, jnp.where(place == 2, rest, 0.0)))
    offset = jnp.sum(
        lax.dot_general(
            slope[...],
            means.astype(jnp.bfloat16),
            (((1,), (1,)), ((), ())),
            preferred_element_type=jnp.float32,
        ),
        axis=1,
        keepdims=True,
    )
    outs = []
    for n in range(samples // WIDE):
        found = lax.dot_general(
            slope[...],
            dosage[n * WIDE : (n + 1) * WIDE, :],
            (((1,), (1,)), ((), ())),
            preferred_element_type=jnp.float32,
        )
        predicted[:, n * WIDE : (n + 1) * WIDE] = (found - offset).astype(jnp.bfloat16)
        copy = pltpu.make_async_copy(
            predicted.at[:, pl.ds(n * WIDE, WIDE)],
            out_hbm.at[:, pl.ds(n * WIDE, WIDE)],
            sems.at[chunks + 3 + n],
        )
        copy.start()
        outs.append(copy)
    for copy in outs:
        copy.wait()


def level_zero(dosage, eigvec, eigval, pheno):
    samples, width = dosage.shape
    traits = pheno.shape[1]
    rows = RIDGES * traits
    anywhere = pl.BlockSpec(memory_space=pl.ANY)
    return pl.pallas_call(
        level_zero_kernel,
        out_shape=jax.ShapeDtypeStruct((rows, samples), jnp.bfloat16),
        in_specs=[anywhere] * 4,
        out_specs=anywhere,
        scratch_shapes=[
            pltpu.VMEM((samples, width), jnp.bfloat16),
            pltpu.VMEM((width, width), jnp.bfloat16),
            pltpu.VMEM((1, width), jnp.float32),
            pltpu.VMEM((samples, traits), jnp.bfloat16),
            pltpu.VMEM((traits + 2 * SUBLANES, width), jnp.float32),
            pltpu.VMEM((1, width), jnp.float32),
            pltpu.VMEM((rows, width), jnp.bfloat16),
            pltpu.VMEM((rows, width), jnp.bfloat16),
            pltpu.VMEM((rows, samples), jnp.bfloat16),
            pltpu.SemaphoreType.DMA((width // TILE + 3 + samples // WIDE,)),
        ],
        compiler_params=pltpu.CompilerParams(vmem_limit_bytes=63 << 20),
        name="level_zero",
    )(dosage, eigvec, eigval, pheno)


def reorder_matrix(traits, blocks, parts):
    size = blocks * RIDGES * traits // parts
    row = lax.broadcasted_iota(jnp.int32, (size, size), 0)
    column = lax.broadcasted_iota(jnp.int32, (size, size), 1)
    group = blocks // parts
    block, rest = row % group, row // group
    ridge, pair = rest % RIDGES, rest // RIDGES
    trait = (pair % 2) * (traits // 2) + pair // 2
    return jnp.where(column == (block * RIDGES + ridge) * traits + trait, 1.0, 0.0).astype(
        jnp.bfloat16
    )


def inverse_two(m):
    (a, b), (c, d) = m
    scale = 1.0 / (a * d - b * c)
    return ((d * scale, -b * scale), (-c * scale, a * scale))


def product(x, y):
    return tuple(
        tuple(x[i][0] * y[0][j] + x[i][1] * y[1][j] for j in range(2)) for i in range(2)
    )


def negative(x):
    return tuple(tuple(-value for value in row) for row in x)


def inverse_four(m):
    def corner(i, j):
        return ((m[i][j], m[i][j + 1]), (m[i + 1][j], m[i + 1][j + 1]))

    first = inverse_two(corner(0, 0))
    left = product(corner(2, 0), first)
    right = product(first, corner(0, 2))
    inner = product(left, corner(0, 2))
    last = corner(2, 2)
    second = inverse_two(
        tuple(tuple(last[i][j] - inner[i][j] for j in range(2)) for i in range(2))
    )
    below = product(second, left)
    back = product(right, below)
    top = tuple(tuple(first[i][j] + back[i][j] for j in range(2)) for i in range(2))
    beside, below = negative(product(right, second)), negative(below)
    return [list(top[i]) + list(beside[i]) for i in range(2)] + [
        list(below[i]) + list(second[i]) for i in range(2)
    ]


def gather_lanes(tile, lanes):
    return jnp.take_along_axis(tile, lanes, axis=1)


def solve(table, span):
    heights, tiles = len(table), len(table[0])
    size = (tiles - 1) * SUBLANES
    lane = lax.broadcasted_iota(jnp.int32, (SUBLANES, LANES), 1)
    within = lane % span

    def eliminate(k, rows, count):
        home, low = k // span, k % span
        first, sub = k // SUBLANES, k % SUBLANES
        pivot = [
            [
                jnp.broadcast_to(rows[m][0][sub + n : sub + n + 1], (SUBLANES, LANES))
                for n in range(4)
            ]
            for m in range(count)
        ]
        inverse = inverse_four(pivot[:4])

        def combine(values):
            return [
                (values[0] * inverse[0][n] + values[1] * inverse[1][n])
                + (values[2] * inverse[2][n] + values[3] * inverse[3][n])
                for n in range(4)
            ]

        def clear(base, factors, r):
            return (
                base
                - (factors[0] * rows[0][r] + factors[1] * rows[1][r])
                - (factors[2] * rows[2][r] + factors[3] * rows[3][r])
            )

        later = []
        for m in range(4, count):
            factors = combine(pivot[m])
            later.append([clear(rows[m][r], factors, r) for r in range(tiles - first)])
        chosen = (within >= low) & (within < low + 4)
        for h in sorted(range(heights), key=lambda h: h != min(k + 4, size - 4) // span):
            factors = combine(
                [
                    jnp.broadcast_to(table[h][first][sub + m : sub + m + 1], (SUBLANES, LANES))
                    for m in range(4)
                ]
            )
            if h == home:
                for n in range(4):
                    for m in range(4):
                        factors[n] = jnp.where(within == low + m, -inverse[m][n], factors[n])
            for r in range(first, tiles):
                base = table[h][r]
                if h == home:
                    base = jnp.where(chosen, 0.0, base)
                table[h][r] = clear(base, factors, r - first)
        return later

    for k in range(0, size, 8):
        lanes = (lane - within) + k % span
        rows = [
            [gather_lanes(table[k // span][r], lanes + m) for r in range(k // SUBLANES, tiles)]
            for m in range(8)
        ]
        eliminate(k + 4, eliminate(k, rows, 8), 4)
    return [table[h][tiles - 1] for h in range(heights)]


def exchange(tiles, span):
    lane = lax.broadcasted_iota(jnp.int32, (SUBLANES, LANES), 1)
    tiles = list(tiles)
    for bit in (1, 2):
        shift = bit * span
        odd = (lane // shift) % 2 == 1
        for i in range(4):
            if not i & bit:
                x, y = tiles[i], tiles[i | bit]
                tiles[i] = jnp.where(odd, pltpu.roll(y, shift, 1), x)
                tiles[i | bit] = jnp.where(odd, y, pltpu.roll(x, LANES - shift, 1))
    return tiles


def newton_kernel(traits, blocks, arrived, target, out, design, lhs, table_ref):
    samples = arrived.shape[1]
    predictors = RIDGES * blocks
    half = traits // 2
    parts = arrived.shape[0] // TILE
    order = reorder_matrix(traits, blocks, parts)
    group = blocks // parts
    for part in range(parts):
        moved = jnp.dot(
            order, arrived[part * TILE : (part + 1) * TILE, :], preferred_element_type=jnp.float32
        )
        for i in range(TILE // group):
            start = i * blocks + part * group
            design[start : start + group, :] = moved[i * group : (i + 1) * group].astype(
                jnp.bfloat16
            )
    level_ridge = LEVEL_ONE * samples
    lane = lax.broadcasted_iota(jnp.int32, (SUBLANES, LANES), 1)
    sub = lax.broadcasted_iota(jnp.int32, (SUBLANES, LANES), 0)
    upper = lane >= predictors
    pheno = target[...]
    middle = predictors + 2 * traits
    rows = predictors // SUBLANES

    def systems(weights):
        if weights is None:
            resid = pheno - 0.5
        else:
            spread_out = [
                jnp.where((lane // predictors) * half + s == sub, w, 0.0).astype(jnp.bfloat16)
                for s, w in enumerate(exchange(weights, blocks))
            ]
            logits = jnp.dot(
                jnp.concatenate(spread_out, axis=1), design[...], preferred_element_type=jnp.float32
            )
            prob = 1.0 / (1.0 + jnp.exp(-logits))
            curve = prob * (1.0 - prob)
            resid = pheno - prob
        resid = jnp.concatenate([resid, jnp.zeros_like(resid)], axis=0).astype(jnp.bfloat16)
        found = []
        for s in range(half):
            base = s * 2 * predictors
            pair = design[base : base + 2 * predictors, :]
            lhs[s, predictors:middle, :] = resid
            for start, trait, place in ((0, s, 0), (predictors, s + half, middle)):
                own = design[base + start : base + start + predictors, :]
                if weights is not None:
                    own = (own.astype(jnp.float32) * curve[trait : trait + 1, :]).astype(
                        jnp.bfloat16
                    )
                lhs[s, place : place + predictors, :] = own
            result = lax.dot_general(
                lhs[s], pair, (((1,), (1,)), ((), ())), preferred_element_type=jnp.float32
            )
            tiles = [
                jnp.where(
                    upper,
                    result[middle + SUBLANES * r : middle + SUBLANES * (r + 1)],
                    result[SUBLANES * r : SUBLANES * (r + 1)],
                )
                for r in range(rows)
            ]
            if weights is None:
                tiles = [tile * 0.25 for tile in tiles]
            first, second = predictors + s, predictors + s + half
            gradient = jnp.where(upper[:1], result[second : second + 1], result[first : first + 1])
            tiles.append(jnp.broadcast_to(gradient, (SUBLANES, LANES)))
            found.append(tiles)
        for r in range(rows + 1):
            for h, tile in enumerate(exchange([found[s][r] for s in range(half)], blocks)):
                if r < rows:
                    same = SUBLANES * r + sub == h * blocks + lane % blocks
                    tile = tile + jnp.where(same, level_ridge, 0.0)
                elif weights is not None:
                    tile = tile - level_ridge * weights[h]
                table_ref[h, r] = tile

    def step(index, weights):
        table = [[table_ref[h, r] for r in range(rows + 1)] for h in range(RIDGES)]
        solved = solve(table, blocks)
        weights = tuple(
            weights[h] + jnp.broadcast_to(solved[h][0:1], (SUBLANES, LANES))
            for h in range(RIDGES)
        )

        @pl.when(index < NEWTON - 1)
        def _():
            systems(weights)

        return weights

    systems(None)
    start = tuple(jnp.zeros((SUBLANES, LANES), jnp.float32) for _ in range(RIDGES))
    weights = lax.fori_loop(0, NEWTON, step, start)
    result = jnp.zeros((SUBLANES, LANES), jnp.float32)
    for s, tile in enumerate(exchange(weights, blocks)):
        result = jnp.where(sub == s, tile, result)
        result = jnp.where(sub == s + half, pltpu.roll(tile, predictors, 1), result)
    out[...] = result[:, :predictors]


def newton(arrived, target, blocks):
    rows, samples = arrived.shape
    traits = target.shape[0]
    predictors = rows // traits
    return pl.pallas_call(
        functools.partial(newton_kernel, traits, blocks),
        out_shape=jax.ShapeDtypeStruct((traits, predictors), jnp.float32),
        in_specs=[pl.BlockSpec(memory_space=pltpu.VMEM)] * 2,
        out_specs=pl.BlockSpec(memory_space=pltpu.VMEM),
        scratch_shapes=[
            pltpu.VMEM((rows, samples), jnp.bfloat16),
            pltpu.VMEM((traits // 2, 2 * predictors + 2 * traits, samples), jnp.bfloat16),
            pltpu.VMEM((RIDGES, predictors // SUBLANES + 1, SUBLANES, LANES), jnp.float32),
        ],
        compiler_params=pltpu.CompilerParams(vmem_limit_bytes=48 << 20),
        name="newton",
    )(arrived, target)


def fit_traits(arrived, target):
    rows, samples = arrived.shape
    count = target.shape[0]
    predictors = rows // count
    design = arrived.reshape(-1, RIDGES, count, samples).transpose(2, 0, 1, 3)
    design = design.reshape(count, predictors, samples)
    level_ridge = LEVEL_ONE * samples
    weights = jnp.zeros((count, predictors), jnp.float32)
    identity = jnp.eye(predictors, dtype=jnp.float32)
    for _ in range(NEWTON):
        logits = jnp.einsum(
            "kqn,kq->kn", design, weights.astype(jnp.bfloat16), preferred_element_type=jnp.float32
        )
        prob = jax.nn.sigmoid(logits)
        resid = (target - prob).astype(jnp.bfloat16)
        weighted = (design * (prob * (1.0 - prob))[:, None, :]).astype(jnp.bfloat16)
        gram = jnp.einsum("kqn,kpn->kqp", weighted, design, preferred_element_type=jnp.float32)
        grad = jnp.einsum("kqn,kn->kq", design, resid, preferred_element_type=jnp.float32)
        grad = grad - level_ridge * weights
        factor = jnp.linalg.cholesky(gram + level_ridge * identity)
        partial_solve = lax.linalg.triangular_solve(
            factor, grad[:, :, None], left_side=True, lower=True
        )
        update = lax.linalg.triangular_solve(
            factor, partial_solve, left_side=True, lower=True, transpose_a=True
        )
        weights = weights + update[:, :, 0]
    return weights.reshape(count, -1, RIDGES).swapaxes(1, 2).reshape(count, predictors)


def on_device(dosage, eigvec, eigval, pheno):
    traits = pheno.shape[1]
    regions = lax.axis_size("region")
    per_device = traits // regions
    predicted = level_zero(dosage, eigvec, eigval, pheno)
    if per_device != SUBLANES:
        predicted = predicted.reshape(-1, RIDGES, SUBLANES // per_device, per_device, dosage.shape[0])
        predicted = predicted.swapaxes(1, 2).reshape(RIDGES * traits, dosage.shape[0])
    arrived = lax.all_to_all(predicted, "region", split_axis=0, concat_axis=0, tiled=True)
    position = lax.axis_index("region")
    target = lax.dynamic_slice_in_dim(pheno, position * per_device, per_device, 1)
    target = target.astype(jnp.float32).T
    if per_device == SUBLANES and per_device * regions == LANES:
        return newton(arrived, target, regions)
    return fit_traits(arrived, target)


def solution(mesh):
    return jax.shard_map(
        on_device,
        mesh=mesh,
        in_specs=(
            P("cohort", "region"),
            P("region", "cohort"),
            P("cohort", "region"),
            P("cohort", None),
        ),
        out_specs=P("region", "cohort"),
        check_vma=False,
    )
```

```python
import functools

import jax
import jax.numpy as jnp
from jax import lax
from jax.experimental import pallas as pl
from jax.experimental.pallas import tpu as pltpu
from jax.sharding import PartitionSpec as P

NEWTON = 3
EPSILON = 1e-05
HERITABILITY = (0.01, 0.25, 0.75, 0.99)
LEVEL_ONE = 0.03125
RIDGES = len(HERITABILITY)
LANES = 128
SUBLANES = 8
TILE = 256
WIDE = 512
HALF = 8


def level_zero_kernel(
    dosage_hbm,
    eigvec_hbm,
    eigval_hbm,
    pheno_hbm,
    place,
    *rest,
):
    count = len(rest) - 10
    outs_hbm, scratch = rest[:count], rest[count:]
    level_zero_body(dosage_hbm, eigvec_hbm, eigval_hbm, pheno_hbm, place, outs_hbm, *scratch)


def level_zero_body(
    dosage_hbm,
    eigvec_hbm,
    eigval_hbm,
    pheno_hbm,
    place,
    outs_hbm,
    dosage,
    eigvec,
    eigval,
    pheno,
    covariance,
    squares,
    scaled,
    slope,
    predicted,
    sems,
):
    samples, width = dosage.shape
    traits = pheno.shape[1]
    chunks = width // TILE
    copies = [
        pltpu.make_async_copy(
            dosage_hbm.at[:, pl.ds(c * TILE, TILE)], dosage.at[:, pl.ds(c * TILE, TILE)], sems.at[c]
        )
        for c in range(chunks)
    ]
    cases_copy = pltpu.make_async_copy(pheno_hbm, pheno, sems.at[chunks])
    basis = pltpu.make_async_copy(eigvec_hbm, eigvec, sems.at[chunks + 1])
    values = pltpu.make_async_copy(eigval_hbm, eigval, sems.at[chunks + 2])
    cases_copy.start()
    for copy in copies:
        copy.start()
    basis.start()
    values.start()

    row = lax.broadcasted_iota(jnp.int32, (traits, traits), 0)
    column = lax.broadcasted_iota(jnp.int32, (traits, traits), 1)
    cases_copy.wait()
    turned = lax.dot_general(
        jnp.where(row == column, 1.0, 0.0).astype(jnp.bfloat16),
        pheno[...],
        (((1,), (1,)), ((), ())),
        preferred_element_type=jnp.float32,
    )
    cases = jnp.sum(turned, axis=1, keepdims=True)
    center = cases / samples
    spread = jnp.sqrt(
        (cases * samples - cases * cases) / (samples * float(samples)) + EPSILON
    )
    ones = ((1.0 - center) / spread).astype(jnp.bfloat16).astype(jnp.float32)
    zeros = ((0.0 - center) / spread).astype(jnp.bfloat16).astype(jnp.float32)
    delta = ones - zeros
    left = jnp.concatenate([turned, jnp.ones((2 * SUBLANES, samples), jnp.float32)], axis=0).astype(
        jnp.bfloat16
    )
    for c in range(chunks):
        copies[c].wait()
        part = dosage[:, c * TILE : (c + 1) * TILE]
        covariance[:, c * TILE : (c + 1) * TILE] = jnp.dot(
            left, part, preferred_element_type=jnp.float32
        )
        square = part * part
        rows = samples
        while rows > 4 * SUBLANES:
            rows //= 2
            square = square[:rows] + square[rows : 2 * rows]
        squares[:, c * TILE : (c + 1) * TILE] = jnp.sum(
            square.astype(jnp.float32), axis=0, keepdims=True
        )
    total = covariance[traits : traits + 1, :]
    mean = total / samples
    deviation = jnp.sqrt(
        (squares[...] * samples - total * total) / (samples * float(samples)) + EPSILON
    )
    inverse = 1.0 / deviation
    cross = (
        (covariance[:traits, :] - cases * mean) * delta * inverse
    ).astype(jnp.bfloat16)
    basis.wait()
    values.wait()
    rotated = jnp.dot(cross, eigvec[...], preferred_element_type=jnp.float32)
    for r, value in enumerate(HERITABILITY):
        shrunk = rotated * (1.0 / (eigval[...] + width * (1.0 - value) / value))
        for g in range(traits // SUBLANES):
            start = (g * RIDGES + r) * SUBLANES
            scaled[start : start + SUBLANES, :] = shrunk[
                g * SUBLANES : (g + 1) * SUBLANES
            ].astype(jnp.bfloat16)
    for c in range(chunks):
        ridge = lax.dot_general(
            scaled[...],
            eigvec[c * TILE : (c + 1) * TILE, :],
            (((1,), (1,)), ((), ())),
            preferred_element_type=jnp.float32,
        )
        slope[:, c * TILE : (c + 1) * TILE] = (
            ridge * inverse[:, c * TILE : (c + 1) * TILE]
        ).astype(jnp.bfloat16)
    high = mean.astype(jnp.bfloat16).astype(jnp.float32)
    low = (mean - high).astype(jnp.bfloat16).astype(jnp.float32)
    rest = mean - high - low
    line = lax.broadcasted_iota(jnp.int32, (2 * SUBLANES, width), 0)
    means = jnp.where(line == 0, high, jnp.where(line == 1, low, jnp.where(line == 2, rest, 0.0)))
    offset = jnp.sum(
        lax.dot_general(
            slope[...],
            means.astype(jnp.bfloat16),
            (((1,), (1,)), ((), ())),
            preferred_element_type=jnp.float32,
        ),
        axis=1,
        keepdims=True,
    )
    outs = []
    for n in range(samples // WIDE):
        found = lax.dot_general(
            slope[...],
            dosage[n * WIDE : (n + 1) * WIDE, :],
            (((1,), (1,)), ((), ())),
            preferred_element_type=jnp.float32,
        )
        predicted[:, n * WIDE : (n + 1) * WIDE] = (found - offset).astype(jnp.bfloat16)
        for i, out in enumerate(outs_hbm):
            height = out.shape[0]
            if len(outs_hbm) == 1:
                first = 0
            elif i == 0:
                first = pl.multiple_of((place[0] // HALF) * height, height)
            else:
                first = pl.multiple_of((place[0] ^ (HALF + i - 1)) * height, height)
            copy = pltpu.make_async_copy(
                predicted.at[pl.ds(first, height), pl.ds(n * WIDE, WIDE)],
                out.at[:, pl.ds(n * WIDE, WIDE)],
                sems.at[chunks + 3 + n * len(outs_hbm) + i],
            )
            copy.start()
            outs.append(copy)
    for copy in outs:
        copy.wait()


def level_zero(dosage, eigvec, eigval, pheno, place, heights):
    samples, width = dosage.shape
    traits = pheno.shape[1]
    rows = RIDGES * traits
    anywhere = pl.BlockSpec(memory_space=pl.ANY)
    copies = width // TILE + 3 + len(heights) * (samples // WIDE)
    return pl.pallas_call(
        level_zero_kernel,
        out_shape=[jax.ShapeDtypeStruct((height, samples), jnp.bfloat16) for height in heights],
        in_specs=[anywhere] * 4 + [pl.BlockSpec(memory_space=pltpu.SMEM)],
        out_specs=[anywhere] * len(heights),
        scratch_shapes=[
            pltpu.VMEM((samples, width), jnp.bfloat16),
            pltpu.VMEM((width, width), jnp.bfloat16),
            pltpu.VMEM((1, width), jnp.float32),
            pltpu.VMEM((samples, traits), jnp.bfloat16),
            pltpu.VMEM((traits + 2 * SUBLANES, width), jnp.float32),
            pltpu.VMEM((1, width), jnp.float32),
            pltpu.VMEM((rows, width), jnp.bfloat16),
            pltpu.VMEM((rows, width), jnp.bfloat16),
            pltpu.VMEM((rows, samples), jnp.bfloat16),
            pltpu.SemaphoreType.DMA((copies,)),
        ],
        compiler_params=pltpu.CompilerParams(vmem_limit_bytes=63 << 20),
        name="level_zero",
    )(dosage, eigvec, eigval, pheno, place)


def reorder_matrix(traits, blocks, parts):
    size = blocks * RIDGES * traits // parts
    row = lax.broadcasted_iota(jnp.int32, (size, size), 0)
    column = lax.broadcasted_iota(jnp.int32, (size, size), 1)
    group = blocks // parts
    block, rest = row % group, row // group
    ridge, pair = rest % RIDGES, rest // RIDGES
    trait = (pair % 2) * (traits // 2) + pair // 2
    return jnp.where(column == (block * RIDGES + ridge) * traits + trait, 1.0, 0.0).astype(
        jnp.bfloat16
    )


def inverse_two(m):
    (a, b), (c, d) = m
    scale = 1.0 / (a * d - b * c)
    return ((d * scale, -b * scale), (-c * scale, a * scale))


def product(x, y):
    return tuple(
        tuple(x[i][0] * y[0][j] + x[i][1] * y[1][j] for j in range(2)) for i in range(2)
    )


def negative(x):
    return tuple(tuple(-value for value in row) for row in x)


def inverse_four(m):
    def corner(i, j):
        return ((m[i][j], m[i][j + 1]), (m[i + 1][j], m[i + 1][j + 1]))

    first = inverse_two(corner(0, 0))
    left = product(corner(2, 0), first)
    right = product(first, corner(0, 2))
    inner = product(left, corner(0, 2))
    last = corner(2, 2)
    second = inverse_two(
        tuple(tuple(last[i][j] - inner[i][j] for j in range(2)) for i in range(2))
    )
    below = product(second, left)
    back = product(right, below)
    top = tuple(tuple(first[i][j] + back[i][j] for j in range(2)) for i in range(2))
    beside, below = negative(product(right, second)), negative(below)
    return [list(top[i]) + list(beside[i]) for i in range(2)] + [
        list(below[i]) + list(second[i]) for i in range(2)
    ]


def gather_lanes(tile, lanes):
    return jnp.take_along_axis(tile, lanes, axis=1)


def solve(table, span):
    heights, tiles = len(table), len(table[0])
    size = (tiles - 1) * SUBLANES
    lane = lax.broadcasted_iota(jnp.int32, (SUBLANES, LANES), 1)
    within = lane % span

    def eliminate(k, rows, count):
        home, low = k // span, k % span
        first, sub = k // SUBLANES, k % SUBLANES
        pivot = [
            [
                jnp.broadcast_to(rows[m][0][sub + n : sub + n + 1], (SUBLANES, LANES))
                for n in range(4)
            ]
            for m in range(count)
        ]
        inverse = inverse_four(pivot[:4])

        def combine(values):
            return [
                (values[0] * inverse[0][n] + values[1] * inverse[1][n])
                + (values[2] * inverse[2][n] + values[3] * inverse[3][n])
                for n in range(4)
            ]

        def clear(base, factors, r):
            return (
                base
                - (factors[0] * rows[0][r] + factors[1] * rows[1][r])
                - (factors[2] * rows[2][r] + factors[3] * rows[3][r])
            )

        later = []
        for m in range(4, count):
            factors = combine(pivot[m])
            later.append([clear(rows[m][r], factors, r) for r in range(tiles - first)])
        chosen = (within >= low) & (within < low + 4)
        for h in sorted(range(heights), key=lambda h: h != min(k + 4, size - 4) // span):
            factors = combine(
                [
                    jnp.broadcast_to(table[h][first][sub + m : sub + m + 1], (SUBLANES, LANES))
                    for m in range(4)
                ]
            )
            if h == home:
                for n in range(4):
                    for m in range(4):
                        factors[n] = jnp.where(within == low + m, -inverse[m][n], factors[n])
            for r in range(first, tiles):
                base = table[h][r]
                if h == home:
                    base = jnp.where(chosen, 0.0, base)
                table[h][r] = clear(base, factors, r - first)
        return later

    for k in range(0, size, 8):
        lanes = (lane - within) + k % span
        rows = [
            [gather_lanes(table[k // span][r], lanes + m) for r in range(k // SUBLANES, tiles)]
            for m in range(8)
        ]
        eliminate(k + 4, eliminate(k, rows, 8), 4)
    return [table[h][tiles - 1] for h in range(heights)]


def exchange(tiles, span):
    lane = lax.broadcasted_iota(jnp.int32, (SUBLANES, LANES), 1)
    tiles = list(tiles)
    for bit in (1, 2):
        shift = bit * span
        odd = (lane // shift) % 2 == 1
        for i in range(4):
            if not i & bit:
                x, y = tiles[i], tiles[i | bit]
                tiles[i] = jnp.where(odd, pltpu.roll(y, shift, 1), x)
                tiles[i | bit] = jnp.where(odd, y, pltpu.roll(x, LANES - shift, 1))
    return tiles


def newton_kernel(traits, blocks, place, near, *rest):
    *far, target, out, design, lhs, table_ref = rest
    samples = near.shape[1]
    predictors = RIDGES * blocks
    half = traits // 2
    parts = 2
    order = reorder_matrix(traits, blocks, parts)
    group = blocks // parts
    for part in range(parts):
        arrived = near[...] if part == 0 else jnp.concatenate([block[...] for block in far], axis=0)
        moved = jnp.dot(order, arrived, preferred_element_type=jnp.float32)
        for i in range(arrived.shape[0] // group):
            start = i * blocks + part * group
            design[start : start + group, :] = moved[i * group : (i + 1) * group].astype(
                jnp.bfloat16
            )
    level_ridge = LEVEL_ONE * samples
    lane = lax.broadcasted_iota(jnp.int32, (SUBLANES, LANES), 1)
    sub = lax.broadcasted_iota(jnp.int32, (SUBLANES, LANES), 0)
    upper = lane >= predictors
    pheno = target[...]
    middle = predictors + 2 * traits
    rows = predictors // SUBLANES

    def systems(weights):
        if weights is None:
            resid = pheno - 0.5
        else:
            spread_out = [
                jnp.where((lane // predictors) * half + s == sub, w, 0.0).astype(jnp.bfloat16)
                for s, w in enumerate(exchange(weights, blocks))
            ]
            logits = jnp.dot(
                jnp.concatenate(spread_out, axis=1), design[...], preferred_element_type=jnp.float32
            )
            prob = 1.0 / (1.0 + jnp.exp(-logits))
            curve = prob * (1.0 - prob)
            resid = pheno - prob
        resid = jnp.concatenate([resid, jnp.zeros_like(resid)], axis=0).astype(jnp.bfloat16)
        found = []
        for s in range(half):
            base = s * 2 * predictors
            pair = design[base : base + 2 * predictors, :]
            lhs[s, predictors:middle, :] = resid
            for start, trait, place in ((0, s, 0), (predictors, s + half, middle)):
                own = design[base + start : base + start + predictors, :]
                if weights is not None:
                    own = (own.astype(jnp.float32) * curve[trait : trait + 1, :]).astype(
                        jnp.bfloat16
                    )
                lhs[s, place : place + predictors, :] = own
            result = lax.dot_general(
                lhs[s], pair, (((1,), (1,)), ((), ())), preferred_element_type=jnp.float32
            )
            tiles = [
                jnp.where(
                    upper,
                    result[middle + SUBLANES * r : middle + SUBLANES * (r + 1)],
                    result[SUBLANES * r : SUBLANES * (r + 1)],
                )
                for r in range(rows)
            ]
            if weights is None:
                tiles = [tile * 0.25 for tile in tiles]
            first, second = predictors + s, predictors + s + half
            gradient = jnp.where(upper[:1], result[second : second + 1], result[first : first + 1])
            tiles.append(jnp.broadcast_to(gradient, (SUBLANES, LANES)))
            found.append(tiles)
        for r in range(rows + 1):
            for h, tile in enumerate(exchange([found[s][r] for s in range(half)], blocks)):
                if r < rows:
                    same = SUBLANES * r + sub == h * blocks + lane % blocks
                    tile = tile + jnp.where(same, level_ridge, 0.0)
                elif weights is not None:
                    tile = tile - level_ridge * weights[h]
                table_ref[h, r] = tile

    def step(index, weights):
        table = [[table_ref[h, r] for r in range(rows + 1)] for h in range(RIDGES)]
        solved = solve(table, blocks)
        weights = tuple(
            weights[h] + jnp.broadcast_to(solved[h][0:1], (SUBLANES, LANES))
            for h in range(RIDGES)
        )

        @pl.when(index < NEWTON - 1)
        def _():
            systems(weights)

        return weights

    systems(None)
    start = tuple(jnp.zeros((SUBLANES, LANES), jnp.float32) for _ in range(RIDGES))
    weights = lax.fori_loop(0, NEWTON, step, start)
    result = jnp.zeros((SUBLANES, LANES), jnp.float32)
    for s, tile in enumerate(exchange(weights, blocks)):
        result = jnp.where(sub == s, tile, result)
        result = jnp.where(sub == s + half, pltpu.roll(tile, predictors, 1), result)
    block = lane % blocks
    own = block // HALF == place[0] // HALF
    source = jnp.where(own, block % HALF, HALF + (block ^ place[0]) % HALF)
    result = gather_lanes(result, (lane - block) + source)
    out[...] = result[:, :predictors]


def newton(place, near, far, target, blocks):
    samples = near.shape[1]
    traits = target.shape[0]
    predictors = RIDGES * blocks
    inside = pl.BlockSpec(memory_space=pltpu.VMEM)
    return pl.pallas_call(
        functools.partial(newton_kernel, traits, blocks),
        out_shape=jax.ShapeDtypeStruct((traits, predictors), jnp.float32),
        in_specs=[pl.BlockSpec(memory_space=pltpu.SMEM)] + [inside] * (len(far) + 2),
        out_specs=inside,
        scratch_shapes=[
            pltpu.VMEM((traits * predictors, samples), jnp.bfloat16),
            pltpu.VMEM((traits // 2, 2 * predictors + 2 * traits, samples), jnp.bfloat16),
            pltpu.VMEM((RIDGES, predictors // SUBLANES + 1, SUBLANES, LANES), jnp.float32),
        ],
        compiler_params=pltpu.CompilerParams(vmem_limit_bytes=48 << 20),
        name="newton",
    )(place, near, *far, target)


def fit_traits(arrived, target):
    rows, samples = arrived.shape
    count = target.shape[0]
    predictors = rows // count
    design = arrived.reshape(-1, RIDGES, count, samples).transpose(2, 0, 1, 3)
    design = design.reshape(count, predictors, samples)
    level_ridge = LEVEL_ONE * samples
    weights = jnp.zeros((count, predictors), jnp.float32)
    identity = jnp.eye(predictors, dtype=jnp.float32)
    for _ in range(NEWTON):
        logits = jnp.einsum(
            "kqn,kq->kn", design, weights.astype(jnp.bfloat16), preferred_element_type=jnp.float32
        )
        prob = jax.nn.sigmoid(logits)
        resid = (target - prob).astype(jnp.bfloat16)
        weighted = (design * (prob * (1.0 - prob))[:, None, :]).astype(jnp.bfloat16)
        gram = jnp.einsum("kqn,kpn->kqp", weighted, design, preferred_element_type=jnp.float32)
        grad = jnp.einsum("kqn,kn->kq", design, resid, preferred_element_type=jnp.float32)
        grad = grad - level_ridge * weights
        factor = jnp.linalg.cholesky(gram + level_ridge * identity)
        partial_solve = lax.linalg.triangular_solve(
            factor, grad[:, :, None], left_side=True, lower=True
        )
        update = lax.linalg.triangular_solve(
            factor, partial_solve, left_side=True, lower=True, transpose_a=True
        )
        weights = weights + update[:, :, 0]
    return weights.reshape(count, -1, RIDGES).swapaxes(1, 2).reshape(count, predictors)


def on_device(dosage, eigvec, eigval, pheno):
    samples = dosage.shape[0]
    traits = pheno.shape[1]
    regions = lax.axis_size("region")
    per_device = traits // regions
    rows = RIDGES * per_device
    position = lax.axis_index("region")
    place = position.astype(jnp.int32).reshape(1)
    target = lax.dynamic_slice_in_dim(pheno, position * per_device, per_device, 1)
    target = target.astype(jnp.float32).T
    if per_device == SUBLANES and regions == 2 * HALF:
        near, *far = level_zero(
            dosage, eigvec, eigval, pheno, place, [HALF * rows] + [rows] * HALF
        )
        halves = [list(range(HALF)), list(range(HALF, 2 * HALF))]
        near = lax.all_to_all(
            near, "region", split_axis=0, concat_axis=0, tiled=True, axis_index_groups=halves
        )
        far = [
            lax.ppermute(block, "region", [(i, i ^ (HALF + j)) for i in range(regions)])
            for j, block in enumerate(far)
        ]
        return newton(place, near, far, target, regions)
    (predicted,) = level_zero(dosage, eigvec, eigval, pheno, place, [RIDGES * traits])
    predicted = predicted.reshape(-1, RIDGES, SUBLANES // per_device, per_device, samples)
    predicted = predicted.swapaxes(1, 2).reshape(RIDGES * traits, samples)
    arrived = lax.all_to_all(predicted, "region", split_axis=0, concat_axis=0, tiled=True)
    return fit_traits(arrived, target)


def solution(mesh):
    return jax.shard_map(
        on_device,
        mesh=mesh,
        in_specs=(
            P("cohort", "region"),
            P("region", "cohort"),
            P("cohort", "region"),
            P("cohort", None),
        ),
        out_specs=P("region", "cohort"),
        check_vma=False,
    )
```

```python
import functools

import jax
import jax.numpy as jnp
from jax import lax
from jax.experimental import pallas as pl
from jax.experimental.pallas import tpu as pltpu
from jax.sharding import PartitionSpec as P

NEWTON = 3
EPSILON = 1e-05
HERITABILITY = (0.01, 0.25, 0.75, 0.99)
LEVEL_ONE = 0.03125
RIDGES = len(HERITABILITY)
LANES = 128
SUBLANES = 8
TILE = 256
WIDE = 512
ORDER = (12, 5, 10, 3, 13, 6, 11, 2, 14, 7, 8, 15, 4, 9, 1)


def level_zero_kernel(
    dosage_hbm,
    eigvec_hbm,
    eigval_hbm,
    pheno_hbm,
    place,
    *rest,
):
    count = len(rest) - 10
    outs_hbm, scratch = rest[:count], rest[count:]
    level_zero_body(dosage_hbm, eigvec_hbm, eigval_hbm, pheno_hbm, place, outs_hbm, *scratch)


def level_zero_body(
    dosage_hbm,
    eigvec_hbm,
    eigval_hbm,
    pheno_hbm,
    place,
    outs_hbm,
    dosage,
    eigvec,
    eigval,
    pheno,
    covariance,
    squares,
    scaled,
    slope,
    predicted,
    sems,
):
    samples, width = dosage.shape
    traits = pheno.shape[1]
    chunks = width // TILE
    copies = [
        pltpu.make_async_copy(
            dosage_hbm.at[:, pl.ds(c * TILE, TILE)], dosage.at[:, pl.ds(c * TILE, TILE)], sems.at[c]
        )
        for c in range(chunks)
    ]
    cases_copy = pltpu.make_async_copy(pheno_hbm, pheno, sems.at[chunks])
    basis = pltpu.make_async_copy(eigvec_hbm, eigvec, sems.at[chunks + 1])
    values = pltpu.make_async_copy(eigval_hbm, eigval, sems.at[chunks + 2])
    cases_copy.start()
    for copy in copies:
        copy.start()
    basis.start()
    values.start()

    row = lax.broadcasted_iota(jnp.int32, (traits, traits), 0)
    column = lax.broadcasted_iota(jnp.int32, (traits, traits), 1)
    cases_copy.wait()
    turned = lax.dot_general(
        jnp.where(row == column, 1.0, 0.0).astype(jnp.bfloat16),
        pheno[...],
        (((1,), (1,)), ((), ())),
        preferred_element_type=jnp.float32,
    )
    cases = jnp.sum(turned, axis=1, keepdims=True)
    center = cases / samples
    spread = jnp.sqrt(
        (cases * samples - cases * cases) / (samples * float(samples)) + EPSILON
    )
    ones = ((1.0 - center) / spread).astype(jnp.bfloat16).astype(jnp.float32)
    zeros = ((0.0 - center) / spread).astype(jnp.bfloat16).astype(jnp.float32)
    delta = ones - zeros
    left = jnp.concatenate([turned, jnp.ones((2 * SUBLANES, samples), jnp.float32)], axis=0).astype(
        jnp.bfloat16
    )
    for c in range(chunks):
        copies[c].wait()
        part = dosage[:, c * TILE : (c + 1) * TILE]
        covariance[:, c * TILE : (c + 1) * TILE] = jnp.dot(
            left, part, preferred_element_type=jnp.float32
        )
        square = part * part
        rows = samples
        while rows > 4 * SUBLANES:
            rows //= 2
            square = square[:rows] + square[rows : 2 * rows]
        squares[:, c * TILE : (c + 1) * TILE] = jnp.sum(
            square.astype(jnp.float32), axis=0, keepdims=True
        )
    total = covariance[traits : traits + 1, :]
    mean = total / samples
    deviation = jnp.sqrt(
        (squares[...] * samples - total * total) / (samples * float(samples)) + EPSILON
    )
    inverse = 1.0 / deviation
    cross = (
        (covariance[:traits, :] - cases * mean) * delta * inverse
    ).astype(jnp.bfloat16)
    basis.wait()
    values.wait()
    rotated = jnp.dot(cross, eigvec[...], preferred_element_type=jnp.float32)
    for r, value in enumerate(HERITABILITY):
        shrunk = rotated * (1.0 / (eigval[...] + width * (1.0 - value) / value))
        for g in range(traits // SUBLANES):
            start = (g * RIDGES + r) * SUBLANES
            scaled[start : start + SUBLANES, :] = shrunk[
                g * SUBLANES : (g + 1) * SUBLANES
            ].astype(jnp.bfloat16)
    for c in range(chunks):
        ridge = lax.dot_general(
            scaled[...],
            eigvec[c * TILE : (c + 1) * TILE, :],
            (((1,), (1,)), ((), ())),
            preferred_element_type=jnp.float32,
        )
        slope[:, c * TILE : (c + 1) * TILE] = (
            ridge * inverse[:, c * TILE : (c + 1) * TILE]
        ).astype(jnp.bfloat16)
    high = mean.astype(jnp.bfloat16).astype(jnp.float32)
    low = (mean - high).astype(jnp.bfloat16).astype(jnp.float32)
    rest = mean - high - low
    line = lax.broadcasted_iota(jnp.int32, (2 * SUBLANES, width), 0)
    means = jnp.where(line == 0, high, jnp.where(line == 1, low, jnp.where(line == 2, rest, 0.0)))
    offset = jnp.sum(
        lax.dot_general(
            slope[...],
            means.astype(jnp.bfloat16),
            (((1,), (1,)), ((), ())),
            preferred_element_type=jnp.float32,
        ),
        axis=1,
        keepdims=True,
    )
    outs = []
    for n in range(samples // WIDE):
        found = lax.dot_general(
            slope[...],
            dosage[n * WIDE : (n + 1) * WIDE, :],
            (((1,), (1,)), ((), ())),
            preferred_element_type=jnp.float32,
        )
        predicted[:, n * WIDE : (n + 1) * WIDE] = (found - offset).astype(jnp.bfloat16)
        for i, out in enumerate(outs_hbm):
            height = out.shape[0]
            first = 0
            if len(outs_hbm) > 1:
                first = pl.multiple_of((place[0] ^ i) * height, height)
            copy = pltpu.make_async_copy(
                predicted.at[pl.ds(first, height), pl.ds(n * WIDE, WIDE)],
                out.at[:, pl.ds(n * WIDE, WIDE)],
                sems.at[chunks + 3 + n * len(outs_hbm) + i],
            )
            copy.start()
            outs.append(copy)
    for copy in outs:
        copy.wait()


def level_zero(dosage, eigvec, eigval, pheno, place, heights):
    samples, width = dosage.shape
    traits = pheno.shape[1]
    rows = RIDGES * traits
    anywhere = pl.BlockSpec(memory_space=pl.ANY)
    copies = width // TILE + 3 + len(heights) * (samples // WIDE)
    return pl.pallas_call(
        level_zero_kernel,
        out_shape=[jax.ShapeDtypeStruct((height, samples), jnp.bfloat16) for height in heights],
        in_specs=[anywhere] * 4 + [pl.BlockSpec(memory_space=pltpu.SMEM)],
        out_specs=[anywhere] * len(heights),
        scratch_shapes=[
            pltpu.VMEM((samples, width), jnp.bfloat16),
            pltpu.VMEM((width, width), jnp.bfloat16),
            pltpu.VMEM((1, width), jnp.float32),
            pltpu.VMEM((samples, traits), jnp.bfloat16),
            pltpu.VMEM((traits + 2 * SUBLANES, width), jnp.float32),
            pltpu.VMEM((1, width), jnp.float32),
            pltpu.VMEM((rows, width), jnp.bfloat16),
            pltpu.VMEM((rows, width), jnp.bfloat16),
            pltpu.VMEM((rows, samples), jnp.bfloat16),
            pltpu.SemaphoreType.DMA((copies,)),
        ],
        compiler_params=pltpu.CompilerParams(vmem_limit_bytes=63 << 20),
        name="level_zero",
    )(dosage, eigvec, eigval, pheno, place)


def reorder_matrix(traits, blocks, parts):
    size = blocks * RIDGES * traits // parts
    row = lax.broadcasted_iota(jnp.int32, (size, size), 0)
    column = lax.broadcasted_iota(jnp.int32, (size, size), 1)
    group = blocks // parts
    block, rest = row % group, row // group
    ridge, pair = rest % RIDGES, rest // RIDGES
    trait = (pair % 2) * (traits // 2) + pair // 2
    return jnp.where(column == (block * RIDGES + ridge) * traits + trait, 1.0, 0.0).astype(
        jnp.bfloat16
    )


def inverse_two(m):
    (a, b), (c, d) = m
    scale = 1.0 / (a * d - b * c)
    return ((d * scale, -b * scale), (-c * scale, a * scale))


def product(x, y):
    return tuple(
        tuple(x[i][0] * y[0][j] + x[i][1] * y[1][j] for j in range(2)) for i in range(2)
    )


def negative(x):
    return tuple(tuple(-value for value in row) for row in x)


def inverse_four(m):
    def corner(i, j):
        return ((m[i][j], m[i][j + 1]), (m[i + 1][j], m[i + 1][j + 1]))

    first = inverse_two(corner(0, 0))
    left = product(corner(2, 0), first)
    right = product(first, corner(0, 2))
    inner = product(left, corner(0, 2))
    last = corner(2, 2)
    second = inverse_two(
        tuple(tuple(last[i][j] - inner[i][j] for j in range(2)) for i in range(2))
    )
    below = product(second, left)
    back = product(right, below)
    top = tuple(tuple(first[i][j] + back[i][j] for j in range(2)) for i in range(2))
    beside, below = negative(product(right, second)), negative(below)
    return [list(top[i]) + list(beside[i]) for i in range(2)] + [
        list(below[i]) + list(second[i]) for i in range(2)
    ]


def gather_lanes(tile, lanes):
    return jnp.take_along_axis(tile, lanes, axis=1)


def solve(table, span):
    heights, tiles = len(table), len(table[0])
    size = (tiles - 1) * SUBLANES
    lane = lax.broadcasted_iota(jnp.int32, (SUBLANES, LANES), 1)
    within = lane % span

    def eliminate(k, rows, count):
        home, low = k // span, k % span
        first, sub = k // SUBLANES, k % SUBLANES
        pivot = [
            [
                jnp.broadcast_to(rows[m][0][sub + n : sub + n + 1], (SUBLANES, LANES))
                for n in range(4)
            ]
            for m in range(count)
        ]
        inverse = inverse_four(pivot[:4])

        def combine(values):
            return [
                (values[0] * inverse[0][n] + values[1] * inverse[1][n])
                + (values[2] * inverse[2][n] + values[3] * inverse[3][n])
                for n in range(4)
            ]

        def clear(base, factors, r):
            return (
                base
                - (factors[0] * rows[0][r] + factors[1] * rows[1][r])
                - (factors[2] * rows[2][r] + factors[3] * rows[3][r])
            )

        later = []
        for m in range(4, count):
            factors = combine(pivot[m])
            later.append([clear(rows[m][r], factors, r) for r in range(tiles - first)])
        chosen = (within >= low) & (within < low + 4)
        for h in sorted(range(heights), key=lambda h: h != min(k + 4, size - 4) // span):
            factors = combine(
                [
                    jnp.broadcast_to(table[h][first][sub + m : sub + m + 1], (SUBLANES, LANES))
                    for m in range(4)
                ]
            )
            if h == home:
                for n in range(4):
                    for m in range(4):
                        factors[n] = jnp.where(within == low + m, -inverse[m][n], factors[n])
            for r in range(first, tiles):
                base = table[h][r]
                if h == home:
                    base = jnp.where(chosen, 0.0, base)
                table[h][r] = clear(base, factors, r - first)
        return later

    for k in range(0, size, 8):
        lanes = (lane - within) + k % span
        rows = [
            [gather_lanes(table[k // span][r], lanes + m) for r in range(k // SUBLANES, tiles)]
            for m in range(8)
        ]
        eliminate(k + 4, eliminate(k, rows, 8), 4)
    return [table[h][tiles - 1] for h in range(heights)]


def exchange(tiles, span):
    lane = lax.broadcasted_iota(jnp.int32, (SUBLANES, LANES), 1)
    tiles = list(tiles)
    for bit in (1, 2):
        shift = bit * span
        odd = (lane // shift) % 2 == 1
        for i in range(4):
            if not i & bit:
                x, y = tiles[i], tiles[i | bit]
                tiles[i] = jnp.where(odd, pltpu.roll(y, shift, 1), x)
                tiles[i | bit] = jnp.where(odd, y, pltpu.roll(x, LANES - shift, 1))
    return tiles


def newton_kernel(traits, blocks, place, *rest):
    *given, target, out, design, lhs, table_ref = rest
    arrays = [given[0]] + [given[1 + ORDER.index(j)] for j in range(1, blocks)]
    samples = target.shape[1]
    predictors = RIDGES * blocks
    half = traits // 2
    parts = 2
    order = reorder_matrix(traits, blocks, parts)
    group = blocks // parts
    for part in range(parts):
        arrived = jnp.concatenate(
            [block[...] for block in arrays[part * group : (part + 1) * group]], axis=0
        )
        moved = jnp.dot(order, arrived, preferred_element_type=jnp.float32)
        for i in range(arrived.shape[0] // group):
            start = i * blocks + part * group
            design[start : start + group, :] = moved[i * group : (i + 1) * group].astype(
                jnp.bfloat16
            )
    level_ridge = LEVEL_ONE * samples
    lane = lax.broadcasted_iota(jnp.int32, (SUBLANES, LANES), 1)
    sub = lax.broadcasted_iota(jnp.int32, (SUBLANES, LANES), 0)
    upper = lane >= predictors
    pheno = target[...]
    middle = predictors + 2 * traits
    rows = predictors // SUBLANES

    def systems(weights):
        if weights is None:
            resid = pheno - 0.5
        else:
            spread_out = [
                jnp.where((lane // predictors) * half + s == sub, w, 0.0).astype(jnp.bfloat16)
                for s, w in enumerate(exchange(weights, blocks))
            ]
            logits = jnp.dot(
                jnp.concatenate(spread_out, axis=1), design[...], preferred_element_type=jnp.float32
            )
            prob = 1.0 / (1.0 + jnp.exp(-logits))
            curve = prob * (1.0 - prob)
            resid = pheno - prob
        resid = jnp.concatenate([resid, jnp.zeros_like(resid)], axis=0).astype(jnp.bfloat16)
        found = []
        for s in range(half):
            base = s * 2 * predictors
            pair = design[base : base + 2 * predictors, :]
            lhs[s, predictors:middle, :] = resid
            for start, trait, place in ((0, s, 0), (predictors, s + half, middle)):
                own = design[base + start : base + start + predictors, :]
                if weights is not None:
                    own = (own.astype(jnp.float32) * curve[trait : trait + 1, :]).astype(
                        jnp.bfloat16
                    )
                lhs[s, place : place + predictors, :] = own
            result = lax.dot_general(
                lhs[s], pair, (((1,), (1,)), ((), ())), preferred_element_type=jnp.float32
            )
            tiles = [
                jnp.where(
                    upper,
                    result[middle + SUBLANES * r : middle + SUBLANES * (r + 1)],
                    result[SUBLANES * r : SUBLANES * (r + 1)],
                )
                for r in range(rows)
            ]
            if weights is None:
                tiles = [tile * 0.25 for tile in tiles]
            first, second = predictors + s, predictors + s + half
            gradient = jnp.where(upper[:1], result[second : second + 1], result[first : first + 1])
            tiles.append(jnp.broadcast_to(gradient, (SUBLANES, LANES)))
            found.append(tiles)
        for r in range(rows + 1):
            for h, tile in enumerate(exchange([found[s][r] for s in range(half)], blocks)):
                if r < rows:
                    same = SUBLANES * r + sub == h * blocks + lane % blocks
                    tile = tile + jnp.where(same, level_ridge, 0.0)
                elif weights is not None:
                    tile = tile - level_ridge * weights[h]
                table_ref[h, r] = tile

    def step(index, weights):
        table = [[table_ref[h, r] for r in range(rows + 1)] for h in range(RIDGES)]
        solved = solve(table, blocks)
        weights = tuple(
            weights[h] + jnp.broadcast_to(solved[h][0:1], (SUBLANES, LANES))
            for h in range(RIDGES)
        )

        @pl.when(index < NEWTON - 1)
        def _():
            systems(weights)

        return weights

    systems(None)
    start = tuple(jnp.zeros((SUBLANES, LANES), jnp.float32) for _ in range(RIDGES))
    weights = lax.fori_loop(0, NEWTON, step, start)
    result = jnp.zeros((SUBLANES, LANES), jnp.float32)
    for s, tile in enumerate(exchange(weights, blocks)):
        result = jnp.where(sub == s, tile, result)
        result = jnp.where(sub == s + half, pltpu.roll(tile, predictors, 1), result)
    block = lane % blocks
    result = gather_lanes(result, (lane - block) + (block ^ place[0]))
    out[...] = result[:, :predictors]


def newton(place, arrays, target, blocks):
    samples = target.shape[1]
    traits = target.shape[0]
    predictors = RIDGES * blocks
    inside = pl.BlockSpec(memory_space=pltpu.VMEM)
    return pl.pallas_call(
        functools.partial(newton_kernel, traits, blocks),
        out_shape=jax.ShapeDtypeStruct((traits, predictors), jnp.float32),
        in_specs=[pl.BlockSpec(memory_space=pltpu.SMEM)] + [inside] * (len(arrays) + 1),
        out_specs=inside,
        scratch_shapes=[
            pltpu.VMEM((traits * predictors, samples), jnp.bfloat16),
            pltpu.VMEM((traits // 2, 2 * predictors + 2 * traits, samples), jnp.bfloat16),
            pltpu.VMEM((RIDGES, predictors // SUBLANES + 1, SUBLANES, LANES), jnp.float32),
        ],
        compiler_params=pltpu.CompilerParams(vmem_limit_bytes=48 << 20),
        name="newton",
    )(place, *arrays, target)


def fit_traits(arrived, target):
    rows, samples = arrived.shape
    count = target.shape[0]
    predictors = rows // count
    design = arrived.reshape(-1, RIDGES, count, samples).transpose(2, 0, 1, 3)
    design = design.reshape(count, predictors, samples)
    level_ridge = LEVEL_ONE * samples
    weights = jnp.zeros((count, predictors), jnp.float32)
    identity = jnp.eye(predictors, dtype=jnp.float32)
    for _ in range(NEWTON):
        logits = jnp.einsum(
            "kqn,kq->kn", design, weights.astype(jnp.bfloat16), preferred_element_type=jnp.float32
        )
        prob = jax.nn.sigmoid(logits)
        resid = (target - prob).astype(jnp.bfloat16)
        weighted = (design * (prob * (1.0 - prob))[:, None, :]).astype(jnp.bfloat16)
        gram = jnp.einsum("kqn,kpn->kqp", weighted, design, preferred_element_type=jnp.float32)
        grad = jnp.einsum("kqn,kn->kq", design, resid, preferred_element_type=jnp.float32)
        grad = grad - level_ridge * weights
        factor = jnp.linalg.cholesky(gram + level_ridge * identity)
        partial_solve = lax.linalg.triangular_solve(
            factor, grad[:, :, None], left_side=True, lower=True
        )
        update = lax.linalg.triangular_solve(
            factor, partial_solve, left_side=True, lower=True, transpose_a=True
        )
        weights = weights + update[:, :, 0]
    return weights.reshape(count, -1, RIDGES).swapaxes(1, 2).reshape(count, predictors)


def on_device(dosage, eigvec, eigval, pheno):
    samples = dosage.shape[0]
    traits = pheno.shape[1]
    regions = lax.axis_size("region")
    per_device = traits // regions
    rows = RIDGES * per_device
    position = lax.axis_index("region")
    place = position.astype(jnp.int32).reshape(1)
    target = lax.dynamic_slice_in_dim(pheno, position * per_device, per_device, 1)
    target = target.astype(jnp.float32).T
    if per_device == SUBLANES and regions == len(ORDER) + 1:
        own, *arrays = level_zero(dosage, eigvec, eigval, pheno, place, [rows] * regions)
        arrays = [
            lax.ppermute(arrays[j - 1], "region", [(i, i ^ j) for i in range(regions)])
            for j in ORDER
        ]
        return newton(place, [own] + arrays, target, regions)
    (predicted,) = level_zero(dosage, eigvec, eigval, pheno, place, [RIDGES * traits])
    predicted = predicted.reshape(-1, RIDGES, SUBLANES // per_device, per_device, samples)
    predicted = predicted.swapaxes(1, 2).reshape(RIDGES * traits, samples)
    arrived = lax.all_to_all(predicted, "region", split_axis=0, concat_axis=0, tiled=True)
    return fit_traits(arrived, target)


def solution(mesh):
    return jax.shard_map(
        on_device,
        mesh=mesh,
        in_specs=(
            P("cohort", "region"),
            P("region", "cohort"),
            P("cohort", "region"),
            P("cohort", None),
        ),
        out_specs=P("region", "cohort"),
        check_vma=False,
    )
```

```python
import functools

import jax
import jax.numpy as jnp
from jax import lax
from jax.experimental import pallas as pl
from jax.experimental.pallas import tpu as pltpu
from jax.sharding import PartitionSpec as P

NEWTON = 3
EPSILON = 1e-05
HERITABILITY = (0.01, 0.25, 0.75, 0.99)
LEVEL_ONE = 0.03125
RIDGES = len(HERITABILITY)
LANES = 128
SUBLANES = 8
TILE = 256
WIDE = 512
ORDER = (12, 5, 10, 3, 13, 6, 11, 2, 14, 7, 8, 15, 4, 9, 1)


def level_zero_kernel(
    dosage_hbm,
    eigvec_hbm,
    eigval_hbm,
    pheno_hbm,
    place,
    *rest,
):
    count = len(rest) - 10
    outs_hbm, scratch = rest[:count], rest[count:]
    level_zero_body(dosage_hbm, eigvec_hbm, eigval_hbm, pheno_hbm, place, outs_hbm, *scratch)


def level_zero_body(
    dosage_hbm,
    eigvec_hbm,
    eigval_hbm,
    pheno_hbm,
    place,
    outs_hbm,
    dosage,
    eigvec,
    eigval,
    pheno,
    covariance,
    squares,
    scaled,
    slope,
    predicted,
    sems,
):
    samples, width = dosage.shape
    traits = pheno.shape[1]
    chunks = width // TILE
    copies = [
        pltpu.make_async_copy(
            dosage_hbm.at[:, pl.ds(c * TILE, TILE)], dosage.at[:, pl.ds(c * TILE, TILE)], sems.at[c]
        )
        for c in range(chunks)
    ]
    cases_copy = pltpu.make_async_copy(pheno_hbm, pheno, sems.at[chunks])
    basis = pltpu.make_async_copy(eigvec_hbm, eigvec, sems.at[chunks + 1])
    values = pltpu.make_async_copy(eigval_hbm, eigval, sems.at[chunks + 2])
    cases_copy.start()
    for copy in copies:
        copy.start()
    basis.start()
    values.start()

    row = lax.broadcasted_iota(jnp.int32, (traits, traits), 0)
    column = lax.broadcasted_iota(jnp.int32, (traits, traits), 1)
    cases_copy.wait()
    turned = lax.dot_general(
        jnp.where(row == column, 1.0, 0.0).astype(jnp.bfloat16),
        pheno[...],
        (((1,), (1,)), ((), ())),
        preferred_element_type=jnp.float32,
    )
    cases = jnp.sum(turned, axis=1, keepdims=True)
    center = cases / samples
    spread = jnp.sqrt(
        (cases * samples - cases * cases) / (samples * float(samples)) + EPSILON
    )
    ones = ((1.0 - center) / spread).astype(jnp.bfloat16).astype(jnp.float32)
    zeros = ((0.0 - center) / spread).astype(jnp.bfloat16).astype(jnp.float32)
    delta = ones - zeros
    left = jnp.concatenate([turned, jnp.ones((2 * SUBLANES, samples), jnp.float32)], axis=0).astype(
        jnp.bfloat16
    )
    for c in range(chunks):
        copies[c].wait()
        part = dosage[:, c * TILE : (c + 1) * TILE]
        covariance[:, c * TILE : (c + 1) * TILE] = jnp.dot(
            left, part, preferred_element_type=jnp.float32
        )
        square = part * part
        rows = samples
        while rows > 4 * SUBLANES:
            rows //= 2
            square = square[:rows] + square[rows : 2 * rows]
        squares[:, c * TILE : (c + 1) * TILE] = jnp.sum(
            square.astype(jnp.float32), axis=0, keepdims=True
        )
    total = covariance[traits : traits + 1, :]
    mean = total / samples
    deviation = jnp.sqrt(
        (squares[...] * samples - total * total) / (samples * float(samples)) + EPSILON
    )
    inverse = 1.0 / deviation
    cross = (
        (covariance[:traits, :] - cases * mean) * delta * inverse
    ).astype(jnp.bfloat16)
    basis.wait()
    values.wait()
    rotated = jnp.dot(cross, eigvec[...], preferred_element_type=jnp.float32)
    for r, value in enumerate(HERITABILITY):
        shrunk = rotated * (1.0 / (eigval[...] + width * (1.0 - value) / value))
        for g in range(traits // SUBLANES):
            start = (g * RIDGES + r) * SUBLANES
            scaled[start : start + SUBLANES, :] = shrunk[
                g * SUBLANES : (g + 1) * SUBLANES
            ].astype(jnp.bfloat16)
    for c in range(chunks):
        ridge = lax.dot_general(
            scaled[...],
            eigvec[c * TILE : (c + 1) * TILE, :],
            (((1,), (1,)), ((), ())),
            preferred_element_type=jnp.float32,
        )
        slope[:, c * TILE : (c + 1) * TILE] = (
            ridge * inverse[:, c * TILE : (c + 1) * TILE]
        ).astype(jnp.bfloat16)
    high = mean.astype(jnp.bfloat16).astype(jnp.float32)
    low = (mean - high).astype(jnp.bfloat16).astype(jnp.float32)
    rest = mean - high - low
    line = lax.broadcasted_iota(jnp.int32, (2 * SUBLANES, width), 0)
    means = jnp.where(line == 0, high, jnp.where(line == 1, low, jnp.where(line == 2, rest, 0.0)))
    offset = jnp.sum(
        lax.dot_general(
            slope[...],
            means.astype(jnp.bfloat16),
            (((1,), (1,)), ((), ())),
            preferred_element_type=jnp.float32,
        ),
        axis=1,
        keepdims=True,
    )
    outs = []
    for n in range(samples // WIDE):
        found = lax.dot_general(
            slope[...],
            dosage[n * WIDE : (n + 1) * WIDE, :],
            (((1,), (1,)), ((), ())),
            preferred_element_type=jnp.float32,
        )
        predicted[:, n * WIDE : (n + 1) * WIDE] = (found - offset).astype(jnp.bfloat16)
        for i, out in enumerate(outs_hbm):
            height = out.shape[0]
            first = 0
            if len(outs_hbm) > 1:
                first = pl.multiple_of((place[0] ^ i) * height, height)
            copy = pltpu.make_async_copy(
                predicted.at[pl.ds(first, height), pl.ds(n * WIDE, WIDE)],
                out.at[:, pl.ds(n * WIDE, WIDE)],
                sems.at[chunks + 3 + n * len(outs_hbm) + i],
            )
            copy.start()
            outs.append(copy)
    for copy in outs:
        copy.wait()


def level_zero(dosage, eigvec, eigval, pheno, place, heights):
    samples, width = dosage.shape
    traits = pheno.shape[1]
    rows = RIDGES * traits
    anywhere = pl.BlockSpec(memory_space=pl.ANY)
    copies = width // TILE + 3 + len(heights) * (samples // WIDE)
    return pl.pallas_call(
        level_zero_kernel,
        out_shape=[jax.ShapeDtypeStruct((height, samples), jnp.bfloat16) for height in heights],
        in_specs=[anywhere] * 4 + [pl.BlockSpec(memory_space=pltpu.SMEM)],
        out_specs=[anywhere] * len(heights),
        scratch_shapes=[
            pltpu.VMEM((samples, width), jnp.bfloat16),
            pltpu.VMEM((width, width), jnp.bfloat16),
            pltpu.VMEM((1, width), jnp.float32),
            pltpu.VMEM((samples, traits), jnp.bfloat16),
            pltpu.VMEM((traits + 2 * SUBLANES, width), jnp.float32),
            pltpu.VMEM((1, width), jnp.float32),
            pltpu.VMEM((rows, width), jnp.bfloat16),
            pltpu.VMEM((rows, width), jnp.bfloat16),
            pltpu.VMEM((rows, samples), jnp.bfloat16),
            pltpu.SemaphoreType.DMA((copies,)),
        ],
        compiler_params=pltpu.CompilerParams(vmem_limit_bytes=63 << 20),
        name="level_zero",
    )(dosage, eigvec, eigval, pheno, place)


def reorder_matrix(traits, blocks, parts):
    size = blocks * RIDGES * traits // parts
    row = lax.broadcasted_iota(jnp.int32, (size, size), 0)
    column = lax.broadcasted_iota(jnp.int32, (size, size), 1)
    group = blocks // parts
    block, rest = row % group, row // group
    ridge, pair = rest % RIDGES, rest // RIDGES
    trait = (pair % 2) * (traits // 2) + pair // 2
    return jnp.where(column == (block * RIDGES + ridge) * traits + trait, 1.0, 0.0).astype(
        jnp.bfloat16
    )


def inverse_two(m):
    (a, b), (c, d) = m
    scale = 1.0 / (a * d - b * c)
    return ((d * scale, -b * scale), (-c * scale, a * scale))


def product(x, y):
    return tuple(
        tuple(x[i][0] * y[0][j] + x[i][1] * y[1][j] for j in range(2)) for i in range(2)
    )


def negative(x):
    return tuple(tuple(-value for value in row) for row in x)


def inverse_four(m):
    def corner(i, j):
        return ((m[i][j], m[i][j + 1]), (m[i + 1][j], m[i + 1][j + 1]))

    first = inverse_two(corner(0, 0))
    left = product(corner(2, 0), first)
    right = product(first, corner(0, 2))
    inner = product(left, corner(0, 2))
    last = corner(2, 2)
    second = inverse_two(
        tuple(tuple(last[i][j] - inner[i][j] for j in range(2)) for i in range(2))
    )
    below = product(second, left)
    back = product(right, below)
    top = tuple(tuple(first[i][j] + back[i][j] for j in range(2)) for i in range(2))
    beside, below = negative(product(right, second)), negative(below)
    return [list(top[i]) + list(beside[i]) for i in range(2)] + [
        list(below[i]) + list(second[i]) for i in range(2)
    ]


def gather_lanes(tile, lanes):
    return jnp.take_along_axis(tile, lanes, axis=1)


def solve(table, span):
    heights, tiles = len(table), len(table[0])
    size = (tiles - 1) * SUBLANES
    lane = lax.broadcasted_iota(jnp.int32, (SUBLANES, LANES), 1)
    within = lane % span

    def eliminate(k, rows, count):
        home, low = k // span, k % span
        first, sub = k // SUBLANES, k % SUBLANES
        pivot = [
            [
                jnp.broadcast_to(rows[m][0][sub + n : sub + n + 1], (SUBLANES, LANES))
                for n in range(4)
            ]
            for m in range(count)
        ]
        inverse = inverse_four(pivot[:4])

        def combine(values):
            return [
                (values[0] * inverse[0][n] + values[1] * inverse[1][n])
                + (values[2] * inverse[2][n] + values[3] * inverse[3][n])
                for n in range(4)
            ]

        def clear(base, factors, r):
            return (
                base
                - (factors[0] * rows[0][r] + factors[1] * rows[1][r])
                - (factors[2] * rows[2][r] + factors[3] * rows[3][r])
            )

        later = []
        for m in range(4, count):
            factors = combine(pivot[m])
            later.append([clear(rows[m][r], factors, r) for r in range(tiles - first)])
        chosen = (within >= low) & (within < low + 4)
        for h in sorted(range(heights), key=lambda h: h != min(k + 4, size - 4) // span):
            factors = combine(
                [
                    jnp.broadcast_to(table[h][first][sub + m : sub + m + 1], (SUBLANES, LANES))
                    for m in range(4)
                ]
            )
            if h == home:
                for n in range(4):
                    for m in range(4):
                        factors[n] = jnp.where(within == low + m, -inverse[m][n], factors[n])
            for r in range(first, tiles):
                base = table[h][r]
                if h == home:
                    base = jnp.where(chosen, 0.0, base)
                table[h][r] = clear(base, factors, r - first)
        return later

    for k in range(0, size, 8):
        lanes = (lane - within) + k % span
        rows = [
            [gather_lanes(table[k // span][r], lanes + m) for r in range(k // SUBLANES, tiles)]
            for m in range(8)
        ]
        eliminate(k + 4, eliminate(k, rows, 8), 4)
    return [table[h][tiles - 1] for h in range(heights)]


def exchange(tiles, span):
    lane = lax.broadcasted_iota(jnp.int32, (SUBLANES, LANES), 1)
    tiles = list(tiles)
    for bit in (1, 2):
        shift = bit * span
        odd = (lane // shift) % 2 == 1
        for i in range(4):
            if not i & bit:
                x, y = tiles[i], tiles[i | bit]
                tiles[i] = jnp.where(odd, pltpu.roll(y, shift, 1), x)
                tiles[i | bit] = jnp.where(odd, y, pltpu.roll(x, LANES - shift, 1))
    return tiles


def newton_kernel(traits, blocks, place, *rest):
    *given, target, out, design, lhs, table_ref = rest
    arrays = [given[0]] + [given[1 + ORDER.index(j)] for j in range(1, blocks)]
    samples = target.shape[1]
    predictors = RIDGES * blocks
    half = traits // 2
    parts = 2
    order = reorder_matrix(traits, blocks, parts)
    group = blocks // parts
    for part in range(parts):
        arrived = jnp.concatenate(
            [block[...] for block in arrays[part * group : (part + 1) * group]], axis=0
        )
        moved = jnp.dot(order, arrived, preferred_element_type=jnp.float32)
        for i in range(arrived.shape[0] // group):
            start = i * blocks + part * group
            design[start : start + group, :] = moved[i * group : (i + 1) * group].astype(
                jnp.bfloat16
            )
    level_ridge = LEVEL_ONE * samples
    lane = lax.broadcasted_iota(jnp.int32, (SUBLANES, LANES), 1)
    sub = lax.broadcasted_iota(jnp.int32, (SUBLANES, LANES), 0)
    upper = lane >= predictors
    pheno = target[...]
    middle = predictors + 2 * traits
    rows = predictors // SUBLANES

    def systems(weights):
        if weights is None:
            resid = pheno - 0.5
        else:
            spread_out = [
                jnp.where((lane // predictors) * half + s == sub, w, 0.0).astype(jnp.bfloat16)
                for s, w in enumerate(exchange(weights, blocks))
            ]
            logits = jnp.dot(
                jnp.concatenate(spread_out, axis=1), design[...], preferred_element_type=jnp.float32
            )
            prob = 1.0 / (1.0 + jnp.exp(-logits))
            curve = prob * (1.0 - prob)
            resid = pheno - prob
        resid = jnp.concatenate([resid, jnp.zeros_like(resid)], axis=0).astype(jnp.bfloat16)
        found = []
        for s in range(half):
            base = s * 2 * predictors
            pair = design[base : base + 2 * predictors, :]
            lhs[s, predictors:middle, :] = resid
            for start, trait, place in ((0, s, 0), (predictors, s + half, middle)):
                own = design[base + start : base + start + predictors, :]
                if weights is not None:
                    own = (own.astype(jnp.float32) * curve[trait : trait + 1, :]).astype(
                        jnp.bfloat16
                    )
                lhs[s, place : place + predictors, :] = own
            result = lax.dot_general(
                lhs[s], pair, (((1,), (1,)), ((), ())), preferred_element_type=jnp.float32
            )
            tiles = [
                jnp.where(
                    upper,
                    result[middle + SUBLANES * r : middle + SUBLANES * (r + 1)],
                    result[SUBLANES * r : SUBLANES * (r + 1)],
                )
                for r in range(rows)
            ]
            if weights is None:
                tiles = [tile * 0.25 for tile in tiles]
            first, second = predictors + s, predictors + s + half
            gradient = jnp.where(upper[:1], result[second : second + 1], result[first : first + 1])
            tiles.append(jnp.broadcast_to(gradient, (SUBLANES, LANES)))
            found.append(tiles)
        for r in range(rows + 1):
            for h, tile in enumerate(exchange([found[s][r] for s in range(half)], blocks)):
                if r < rows:
                    same = SUBLANES * r + sub == h * blocks + lane % blocks
                    tile = tile + jnp.where(same, level_ridge, 0.0)
                elif weights is not None:
                    tile = tile - level_ridge * weights[h]
                table_ref[h, r] = tile

    def step(index, weights):
        table = [[table_ref[h, r] for r in range(rows + 1)] for h in range(RIDGES)]
        solved = solve(table, blocks)
        weights = tuple(
            weights[h] + jnp.broadcast_to(solved[h][0:1], (SUBLANES, LANES))
            for h in range(RIDGES)
        )

        @pl.when(index < NEWTON - 1)
        def _():
            systems(weights)

        return weights

    systems(None)
    start = tuple(jnp.zeros((SUBLANES, LANES), jnp.float32) for _ in range(RIDGES))
    weights = lax.fori_loop(0, NEWTON, step, start)
    result = jnp.zeros((SUBLANES, LANES), jnp.float32)
    for s, tile in enumerate(exchange(weights, blocks)):
        result = jnp.where(sub == s, tile, result)
        result = jnp.where(sub == s + half, pltpu.roll(tile, predictors, 1), result)
    block = lane % blocks
    result = gather_lanes(result, (lane - block) + (block ^ place[0]))
    out[...] = result[:, :predictors]


def newton(place, arrays, target, blocks):
    samples = target.shape[1]
    traits = target.shape[0]
    predictors = RIDGES * blocks
    inside = pl.BlockSpec(memory_space=pltpu.VMEM)
    return pl.pallas_call(
        functools.partial(newton_kernel, traits, blocks),
        out_shape=jax.ShapeDtypeStruct((traits, predictors), jnp.float32),
        in_specs=[pl.BlockSpec(memory_space=pltpu.SMEM)] + [inside] * (len(arrays) + 1),
        out_specs=inside,
        scratch_shapes=[
            pltpu.VMEM((traits * predictors, samples), jnp.bfloat16),
            pltpu.VMEM((traits // 2, 2 * predictors + 2 * traits, samples), jnp.bfloat16),
            pltpu.VMEM((RIDGES, predictors // SUBLANES + 1, SUBLANES, LANES), jnp.float32),
        ],
        compiler_params=pltpu.CompilerParams(vmem_limit_bytes=48 << 20),
        name="newton",
    )(place, *arrays, target)


def fetch_kernel(block, out):
    out[...] = block[...]


def fetch(block):
    inside = pl.BlockSpec(memory_space=pltpu.VMEM)
    return pl.pallas_call(
        fetch_kernel,
        out_shape=jax.ShapeDtypeStruct(block.shape, block.dtype),
        in_specs=[inside],
        out_specs=inside,
        cost_estimate=pl.CostEstimate(
            flops=0, bytes_accessed=4 * block.size, transcendentals=0
        ),
        compiler_params=pltpu.CompilerParams(vmem_limit_bytes=2 << 20),
        name="fetch",
    )(block)


def fit_traits(arrived, target):
    rows, samples = arrived.shape
    count = target.shape[0]
    predictors = rows // count
    design = arrived.reshape(-1, RIDGES, count, samples).transpose(2, 0, 1, 3)
    design = design.reshape(count, predictors, samples)
    level_ridge = LEVEL_ONE * samples
    weights = jnp.zeros((count, predictors), jnp.float32)
    identity = jnp.eye(predictors, dtype=jnp.float32)
    for _ in range(NEWTON):
        logits = jnp.einsum(
            "kqn,kq->kn", design, weights.astype(jnp.bfloat16), preferred_element_type=jnp.float32
        )
        prob = jax.nn.sigmoid(logits)
        resid = (target - prob).astype(jnp.bfloat16)
        weighted = (design * (prob * (1.0 - prob))[:, None, :]).astype(jnp.bfloat16)
        gram = jnp.einsum("kqn,kpn->kqp", weighted, design, preferred_element_type=jnp.float32)
        grad = jnp.einsum("kqn,kn->kq", design, resid, preferred_element_type=jnp.float32)
        grad = grad - level_ridge * weights
        factor = jnp.linalg.cholesky(gram + level_ridge * identity)
        partial_solve = lax.linalg.triangular_solve(
            factor, grad[:, :, None], left_side=True, lower=True
        )
        update = lax.linalg.triangular_solve(
            factor, partial_solve, left_side=True, lower=True, transpose_a=True
        )
        weights = weights + update[:, :, 0]
    return weights.reshape(count, -1, RIDGES).swapaxes(1, 2).reshape(count, predictors)


def on_device(dosage, eigvec, eigval, pheno):
    samples = dosage.shape[0]
    traits = pheno.shape[1]
    regions = lax.axis_size("region")
    per_device = traits // regions
    rows = RIDGES * per_device
    position = lax.axis_index("region")
    place = position.astype(jnp.int32).reshape(1)
    target = lax.dynamic_slice_in_dim(pheno, position * per_device, per_device, 1)
    target = target.astype(jnp.float32).T
    if per_device == SUBLANES and regions == len(ORDER) + 1:
        own, *arrays = level_zero(dosage, eigvec, eigval, pheno, place, [rows] * regions)
        arrays = [
            lax.ppermute(arrays[j - 1], "region", [(i, i ^ j) for i in range(regions)])
            for j in ORDER
        ]
        return newton(place, [fetch(own)] + arrays, target, regions)
    (predicted,) = level_zero(dosage, eigvec, eigval, pheno, place, [RIDGES * traits])
    predicted = predicted.reshape(-1, RIDGES, SUBLANES // per_device, per_device, samples)
    predicted = predicted.swapaxes(1, 2).reshape(RIDGES * traits, samples)
    arrived = lax.all_to_all(predicted, "region", split_axis=0, concat_axis=0, tiled=True)
    return fit_traits(arrived, target)


def solution(mesh):
    return jax.shard_map(
        on_device,
        mesh=mesh,
        in_specs=(
            P("cohort", "region"),
            P("region", "cohort"),
            P("cohort", "region"),
            P("cohort", None),
        ),
        out_specs=P("region", "cohort"),
        check_vma=False,
    )
```

```python
import functools

import jax
import jax.numpy as jnp
from jax import lax
from jax.experimental import pallas as pl
from jax.experimental.pallas import tpu as pltpu
from jax.sharding import PartitionSpec as P

NEWTON = 3
EPSILON = 1e-05
HERITABILITY = (0.01, 0.25, 0.75, 0.99)
LEVEL_ONE = 0.03125
RIDGES = len(HERITABILITY)
LANES = 128
SUBLANES = 8
TILE = 256
WIDE = 512
ORDER = (12, 5, 10, 3, 13, 6, 11, 2, 14, 7, 8, 15, 4, 9, 1)


def level_zero_kernel(
    dosage_hbm,
    eigvec_hbm,
    eigval_hbm,
    pheno_hbm,
    place,
    *rest,
):
    count = len(rest) - 10
    outs_hbm, scratch = rest[:count], rest[count:]
    level_zero_body(dosage_hbm, eigvec_hbm, eigval_hbm, pheno_hbm, place, outs_hbm, *scratch)


def level_zero_body(
    dosage_hbm,
    eigvec_hbm,
    eigval_hbm,
    pheno_hbm,
    place,
    outs_hbm,
    dosage,
    eigvec,
    eigval,
    pheno,
    covariance,
    squares,
    scaled,
    slope,
    predicted,
    sems,
):
    samples, width = dosage.shape
    traits = pheno.shape[1]
    chunks = width // TILE
    copies = [
        pltpu.make_async_copy(
            dosage_hbm.at[:, pl.ds(c * TILE, TILE)], dosage.at[:, pl.ds(c * TILE, TILE)], sems.at[c]
        )
        for c in range(chunks)
    ]
    cases_copy = pltpu.make_async_copy(pheno_hbm, pheno, sems.at[chunks])
    basis = pltpu.make_async_copy(eigvec_hbm, eigvec, sems.at[chunks + 1])
    values = pltpu.make_async_copy(eigval_hbm, eigval, sems.at[chunks + 2])
    cases_copy.start()
    for copy in copies:
        copy.start()
    basis.start()
    values.start()

    row = lax.broadcasted_iota(jnp.int32, (traits, traits), 0)
    column = lax.broadcasted_iota(jnp.int32, (traits, traits), 1)
    cases_copy.wait()
    turned = lax.dot_general(
        jnp.where(row == column, 1.0, 0.0).astype(jnp.bfloat16),
        pheno[...],
        (((1,), (1,)), ((), ())),
        preferred_element_type=jnp.float32,
    )
    cases = jnp.sum(turned, axis=1, keepdims=True)
    center = cases / samples
    spread = jnp.sqrt(
        (cases * samples - cases * cases) / (samples * float(samples)) + EPSILON
    )
    ones = ((1.0 - center) / spread).astype(jnp.bfloat16).astype(jnp.float32)
    zeros = ((0.0 - center) / spread).astype(jnp.bfloat16).astype(jnp.float32)
    delta = ones - zeros
    left = jnp.concatenate([turned, jnp.ones((2 * SUBLANES, samples), jnp.float32)], axis=0).astype(
        jnp.bfloat16
    )
    for c in range(chunks):
        copies[c].wait()
        part = dosage[:, c * TILE : (c + 1) * TILE]
        covariance[:, c * TILE : (c + 1) * TILE] = jnp.dot(
            left, part, preferred_element_type=jnp.float32
        )
        square = part * part
        rows = samples
        while rows > 4 * SUBLANES:
            rows //= 2
            square = square[:rows] + square[rows : 2 * rows]
        squares[:, c * TILE : (c + 1) * TILE] = jnp.sum(
            square.astype(jnp.float32), axis=0, keepdims=True
        )
    total = covariance[traits : traits + 1, :]
    mean = total / samples
    deviation = jnp.sqrt(
        (squares[...] * samples - total * total) / (samples * float(samples)) + EPSILON
    )
    inverse = 1.0 / deviation
    cross = (
        (covariance[:traits, :] - cases * mean) * delta * inverse
    ).astype(jnp.bfloat16)
    basis.wait()
    values.wait()
    rotated = jnp.dot(cross, eigvec[...], preferred_element_type=jnp.float32)
    for r, value in enumerate(HERITABILITY):
        shrunk = rotated * (1.0 / (eigval[...] + width * (1.0 - value) / value))
        for g in range(traits // SUBLANES):
            start = (g * RIDGES + r) * SUBLANES
            scaled[start : start + SUBLANES, :] = shrunk[
                g * SUBLANES : (g + 1) * SUBLANES
            ].astype(jnp.bfloat16)
    for c in range(chunks):
        ridge = lax.dot_general(
            scaled[...],
            eigvec[c * TILE : (c + 1) * TILE, :],
            (((1,), (1,)), ((), ())),
            preferred_element_type=jnp.float32,
        )
        slope[:, c * TILE : (c + 1) * TILE] = (
            ridge * inverse[:, c * TILE : (c + 1) * TILE]
        ).astype(jnp.bfloat16)
    high = mean.astype(jnp.bfloat16).astype(jnp.float32)
    low = (mean - high).astype(jnp.bfloat16).astype(jnp.float32)
    rest = mean - high - low
    line = lax.broadcasted_iota(jnp.int32, (2 * SUBLANES, width), 0)
    means = jnp.where(line == 0, high, jnp.where(line == 1, low, jnp.where(line == 2, rest, 0.0)))
    offset = jnp.sum(
        lax.dot_general(
            slope[...],
            means.astype(jnp.bfloat16),
            (((1,), (1,)), ((), ())),
            preferred_element_type=jnp.float32,
        ),
        axis=1,
        keepdims=True,
    )
    outs = []
    for n in range(samples // WIDE):
        found = lax.dot_general(
            slope[...],
            dosage[n * WIDE : (n + 1) * WIDE, :],
            (((1,), (1,)), ((), ())),
            preferred_element_type=jnp.float32,
        )
        predicted[:, n * WIDE : (n + 1) * WIDE] = (found - offset).astype(jnp.bfloat16)
        for i, out in enumerate(outs_hbm):
            height = out.shape[0]
            first = 0
            if len(outs_hbm) > 1:
                first = pl.multiple_of((place[0] ^ i) * height, height)
            copy = pltpu.make_async_copy(
                predicted.at[pl.ds(first, height), pl.ds(n * WIDE, WIDE)],
                out.at[:, pl.ds(n * WIDE, WIDE)],
                sems.at[chunks + 3 + n * len(outs_hbm) + i],
            )
            copy.start()
            outs.append(copy)
    for copy in outs:
        copy.wait()


def level_zero(dosage, eigvec, eigval, pheno, place, heights):
    samples, width = dosage.shape
    traits = pheno.shape[1]
    rows = RIDGES * traits
    anywhere = pl.BlockSpec(memory_space=pl.ANY)
    copies = width // TILE + 3 + len(heights) * (samples // WIDE)
    return pl.pallas_call(
        level_zero_kernel,
        out_shape=[jax.ShapeDtypeStruct((height, samples), jnp.bfloat16) for height in heights],
        in_specs=[anywhere] * 4 + [pl.BlockSpec(memory_space=pltpu.SMEM)],
        out_specs=[anywhere] * len(heights),
        scratch_shapes=[
            pltpu.VMEM((samples, width), jnp.bfloat16),
            pltpu.VMEM((width, width), jnp.bfloat16),
            pltpu.VMEM((1, width), jnp.float32),
            pltpu.VMEM((samples, traits), jnp.bfloat16),
            pltpu.VMEM((traits + 2 * SUBLANES, width), jnp.float32),
            pltpu.VMEM((1, width), jnp.float32),
            pltpu.VMEM((rows, width), jnp.bfloat16),
            pltpu.VMEM((rows, width), jnp.bfloat16),
            pltpu.VMEM((rows, samples), jnp.bfloat16),
            pltpu.SemaphoreType.DMA((copies,)),
        ],
        compiler_params=pltpu.CompilerParams(vmem_limit_bytes=63 << 20),
        name="level_zero",
    )(dosage, eigvec, eigval, pheno, place)


def reorder_matrix(traits, blocks, parts):
    size = blocks * RIDGES * traits // parts
    row = lax.broadcasted_iota(jnp.int32, (size, size), 0)
    column = lax.broadcasted_iota(jnp.int32, (size, size), 1)
    group = blocks // parts
    block, rest = row % group, row // group
    ridge, pair = rest % RIDGES, rest // RIDGES
    trait = (pair % 2) * (traits // 2) + pair // 2
    return jnp.where(column == (block * RIDGES + ridge) * traits + trait, 1.0, 0.0).astype(
        jnp.bfloat16
    )


def inverse_two(m):
    (a, b), (c, d) = m
    scale = 1.0 / (a * d - b * c)
    return ((d * scale, -b * scale), (-c * scale, a * scale))


def product(x, y):
    return tuple(
        tuple(x[i][0] * y[0][j] + x[i][1] * y[1][j] for j in range(2)) for i in range(2)
    )


def negative(x):
    return tuple(tuple(-value for value in row) for row in x)


def inverse_four(m):
    def corner(i, j):
        return ((m[i][j], m[i][j + 1]), (m[i + 1][j], m[i + 1][j + 1]))

    first = inverse_two(corner(0, 0))
    left = product(corner(2, 0), first)
    right = product(first, corner(0, 2))
    inner = product(left, corner(0, 2))
    last = corner(2, 2)
    second = inverse_two(
        tuple(tuple(last[i][j] - inner[i][j] for j in range(2)) for i in range(2))
    )
    below = product(second, left)
    back = product(right, below)
    top = tuple(tuple(first[i][j] + back[i][j] for j in range(2)) for i in range(2))
    beside, below = negative(product(right, second)), negative(below)
    return [list(top[i]) + list(beside[i]) for i in range(2)] + [
        list(below[i]) + list(second[i]) for i in range(2)
    ]


def gather_lanes(tile, lanes):
    return jnp.take_along_axis(tile, lanes, axis=1)


def solve(table, span):
    heights, tiles = len(table), len(table[0])
    size = (tiles - 1) * SUBLANES
    lane = lax.broadcasted_iota(jnp.int32, (SUBLANES, LANES), 1)
    within = lane % span

    def eliminate(k, rows, count):
        home, low = k // span, k % span
        first, sub = k // SUBLANES, k % SUBLANES
        pivot = [
            [
                jnp.broadcast_to(rows[m][0][sub + n : sub + n + 1], (SUBLANES, LANES))
                for n in range(4)
            ]
            for m in range(count)
        ]
        inverse = inverse_four(pivot[:4])

        def combine(values):
            return [
                (values[0] * inverse[0][n] + values[1] * inverse[1][n])
                + (values[2] * inverse[2][n] + values[3] * inverse[3][n])
                for n in range(4)
            ]

        def clear(base, factors, r):
            return (
                base
                - (factors[0] * rows[0][r] + factors[1] * rows[1][r])
                - (factors[2] * rows[2][r] + factors[3] * rows[3][r])
            )

        later = []
        for m in range(4, count):
            factors = combine(pivot[m])
            later.append([clear(rows[m][r], factors, r) for r in range(tiles - first)])
        chosen = (within >= low) & (within < low + 4)
        for h in sorted(range(heights), key=lambda h: h != min(k + 4, size - 4) // span):
            factors = combine(
                [
                    jnp.broadcast_to(table[h][first][sub + m : sub + m + 1], (SUBLANES, LANES))
                    for m in range(4)
                ]
            )
            if h == home:
                for n in range(4):
                    for m in range(4):
                        factors[n] = jnp.where(within == low + m, -inverse[m][n], factors[n])
            for r in range(first, tiles):
                base = table[h][r]
                if h == home:
                    base = jnp.where(chosen, 0.0, base)
                table[h][r] = clear(base, factors, r - first)
        return later

    for k in range(0, size, 8):
        lanes = (lane - within) + k % span
        rows = [
            [gather_lanes(table[k // span][r], lanes + m) for r in range(k // SUBLANES, tiles)]
            for m in range(8)
        ]
        eliminate(k + 4, eliminate(k, rows, 8), 4)
    return [table[h][tiles - 1] for h in range(heights)]


def exchange(tiles, span):
    lane = lax.broadcasted_iota(jnp.int32, (SUBLANES, LANES), 1)
    tiles = list(tiles)
    for bit in (1, 2):
        shift = bit * span
        odd = (lane // shift) % 2 == 1
        for i in range(4):
            if not i & bit:
                x, y = tiles[i], tiles[i | bit]
                tiles[i] = jnp.where(odd, pltpu.roll(y, shift, 1), x)
                tiles[i | bit] = jnp.where(odd, y, pltpu.roll(x, LANES - shift, 1))
    return tiles


def newton_kernel(traits, blocks, place, *rest):
    *given, target, out, design, lhs = rest
    arrays = [given[0]] + [given[1 + ORDER.index(j)] for j in range(1, blocks)]
    samples = target.shape[1]
    predictors = RIDGES * blocks
    half = traits // 2
    parts = 2
    order = reorder_matrix(traits, blocks, parts)
    group = blocks // parts
    for part in range(parts):
        arrived = jnp.concatenate(
            [block[...] for block in arrays[part * group : (part + 1) * group]], axis=0
        )
        moved = jnp.dot(order, arrived, preferred_element_type=jnp.float32)
        for i in range(arrived.shape[0] // group):
            start = i * blocks + part * group
            design[start : start + group, :] = moved[i * group : (i + 1) * group].astype(
                jnp.bfloat16
            )
    level_ridge = LEVEL_ONE * samples
    lane = lax.broadcasted_iota(jnp.int32, (SUBLANES, LANES), 1)
    sub = lax.broadcasted_iota(jnp.int32, (SUBLANES, LANES), 0)
    upper = lane >= predictors
    pheno = target[...]
    middle = predictors + 2 * traits
    rows = predictors // SUBLANES

    def systems(weights):
        if weights is None:
            resid = pheno - 0.5
        else:
            spread_out = [
                jnp.where((lane // predictors) * half + s == sub, w, 0.0).astype(jnp.bfloat16)
                for s, w in enumerate(exchange(weights, blocks))
            ]
            logits = jnp.dot(
                jnp.concatenate(spread_out, axis=1), design[...], preferred_element_type=jnp.float32
            )
            prob = 1.0 / (1.0 + jnp.exp(-logits))
            curve = prob * (1.0 - prob)
            resid = pheno - prob
        resid = jnp.concatenate([resid, jnp.zeros_like(resid)], axis=0).astype(jnp.bfloat16)
        found = []
        for s in range(half):
            base = s * 2 * predictors
            pair = design[base : base + 2 * predictors, :]
            lhs[s, predictors:middle, :] = resid
            for start, trait, place in ((0, s, 0), (predictors, s + half, middle)):
                own = design[base + start : base + start + predictors, :]
                if weights is not None:
                    own = (own.astype(jnp.float32) * curve[trait : trait + 1, :]).astype(
                        jnp.bfloat16
                    )
                lhs[s, place : place + predictors, :] = own
            result = lax.dot_general(
                lhs[s], pair, (((1,), (1,)), ((), ())), preferred_element_type=jnp.float32
            )
            tiles = [
                jnp.where(
                    upper,
                    result[middle + SUBLANES * r : middle + SUBLANES * (r + 1)],
                    result[SUBLANES * r : SUBLANES * (r + 1)],
                )
                for r in range(rows)
            ]
            if weights is None:
                tiles = [tile * 0.25 for tile in tiles]
            first, second = predictors + s, predictors + s + half
            gradient = jnp.where(upper[:1], result[second : second + 1], result[first : first + 1])
            tiles.append(jnp.broadcast_to(gradient, (SUBLANES, LANES)))
            found.append(tiles)
        table = [[] for _ in range(RIDGES)]
        for r in range(rows + 1):
            for h, tile in enumerate(exchange([found[s][r] for s in range(half)], blocks)):
                if r < rows:
                    same = SUBLANES * r + sub == h * blocks + lane % blocks
                    tile = tile + jnp.where(same, level_ridge, 0.0)
                elif weights is not None:
                    tile = tile - level_ridge * weights[h]
                table[h].append(tile)
        return table

    table = systems(None)
    weights = tuple(jnp.zeros((SUBLANES, LANES), jnp.float32) for _ in range(RIDGES))
    for index in range(NEWTON):
        solved = solve(table, blocks)
        weights = tuple(
            weights[h] + jnp.broadcast_to(solved[h][0:1], (SUBLANES, LANES))
            for h in range(RIDGES)
        )
        if index < NEWTON - 1:
            table = systems(weights)
    result = jnp.zeros((SUBLANES, LANES), jnp.float32)
    for s, tile in enumerate(exchange(weights, blocks)):
        result = jnp.where(sub == s, tile, result)
        result = jnp.where(sub == s + half, pltpu.roll(tile, predictors, 1), result)
    block = lane % blocks
    result = gather_lanes(result, (lane - block) + (block ^ place[0]))
    out[...] = result[:, :predictors]


def newton(place, arrays, target, blocks):
    samples = target.shape[1]
    traits = target.shape[0]
    predictors = RIDGES * blocks
    inside = pl.BlockSpec(memory_space=pltpu.VMEM)
    return pl.pallas_call(
        functools.partial(newton_kernel, traits, blocks),
        out_shape=jax.ShapeDtypeStruct((traits, predictors), jnp.float32),
        in_specs=[pl.BlockSpec(memory_space=pltpu.SMEM)] + [inside] * (len(arrays) + 1),
        out_specs=inside,
        scratch_shapes=[
            pltpu.VMEM((traits * predictors, samples), jnp.bfloat16),
            pltpu.VMEM((traits // 2, 2 * predictors + 2 * traits, samples), jnp.bfloat16),
        ],
        compiler_params=pltpu.CompilerParams(vmem_limit_bytes=48 << 20),
        name="newton",
    )(place, *arrays, target)


def fetch_kernel(block, out):
    out[...] = block[...]


def fetch(block):
    inside = pl.BlockSpec(memory_space=pltpu.VMEM)
    return pl.pallas_call(
        fetch_kernel,
        out_shape=jax.ShapeDtypeStruct(block.shape, block.dtype),
        in_specs=[inside],
        out_specs=inside,
        cost_estimate=pl.CostEstimate(
            flops=0, bytes_accessed=4 * block.size, transcendentals=0
        ),
        compiler_params=pltpu.CompilerParams(vmem_limit_bytes=2 << 20),
        name="fetch",
    )(block)


def fit_traits(arrived, target):
    rows, samples = arrived.shape
    count = target.shape[0]
    predictors = rows // count
    design = arrived.reshape(-1, RIDGES, count, samples).transpose(2, 0, 1, 3)
    design = design.reshape(count, predictors, samples)
    level_ridge = LEVEL_ONE * samples
    weights = jnp.zeros((count, predictors), jnp.float32)
    identity = jnp.eye(predictors, dtype=jnp.float32)
    for _ in range(NEWTON):
        logits = jnp.einsum(
            "kqn,kq->kn", design, weights.astype(jnp.bfloat16), preferred_element_type=jnp.float32
        )
        prob = jax.nn.sigmoid(logits)
        resid = (target - prob).astype(jnp.bfloat16)
        weighted = (design * (prob * (1.0 - prob))[:, None, :]).astype(jnp.bfloat16)
        gram = jnp.einsum("kqn,kpn->kqp", weighted, design, preferred_element_type=jnp.float32)
        grad = jnp.einsum("kqn,kn->kq", design, resid, preferred_element_type=jnp.float32)
        grad = grad - level_ridge * weights
        factor = jnp.linalg.cholesky(gram + level_ridge * identity)
        partial_solve = lax.linalg.triangular_solve(
            factor, grad[:, :, None], left_side=True, lower=True
        )
        update = lax.linalg.triangular_solve(
            factor, partial_solve, left_side=True, lower=True, transpose_a=True
        )
        weights = weights + update[:, :, 0]
    return weights.reshape(count, -1, RIDGES).swapaxes(1, 2).reshape(count, predictors)


def on_device(dosage, eigvec, eigval, pheno):
    samples = dosage.shape[0]
    traits = pheno.shape[1]
    regions = lax.axis_size("region")
    per_device = traits // regions
    rows = RIDGES * per_device
    position = lax.axis_index("region")
    place = position.astype(jnp.int32).reshape(1)
    target = lax.dynamic_slice_in_dim(pheno, position * per_device, per_device, 1)
    target = target.astype(jnp.float32).T
    if per_device == SUBLANES and regions == len(ORDER) + 1:
        own, *arrays = level_zero(dosage, eigvec, eigval, pheno, place, [rows] * regions)
        arrays = [
            lax.ppermute(arrays[j - 1], "region", [(i, i ^ j) for i in range(regions)])
            for j in ORDER
        ]
        return newton(place, [fetch(own)] + arrays, target, regions)
    (predicted,) = level_zero(dosage, eigvec, eigval, pheno, place, [RIDGES * traits])
    predicted = predicted.reshape(-1, RIDGES, SUBLANES // per_device, per_device, samples)
    predicted = predicted.swapaxes(1, 2).reshape(RIDGES * traits, samples)
    arrived = lax.all_to_all(predicted, "region", split_axis=0, concat_axis=0, tiled=True)
    return fit_traits(arrived, target)


def solution(mesh):
    return jax.shard_map(
        on_device,
        mesh=mesh,
        in_specs=(
            P("cohort", "region"),
            P("region", "cohort"),
            P("cohort", "region"),
            P("cohort", None),
        ),
        out_specs=P("region", "cohort"),
        check_vma=False,
    )
```

```python
import functools

import jax
import jax.numpy as jnp
from jax import lax
from jax.experimental import pallas as pl
from jax.experimental.pallas import tpu as pltpu
from jax.sharding import PartitionSpec as P

NEWTON = 3
EPSILON = 1e-05
HERITABILITY = (0.01, 0.25, 0.75, 0.99)
LEVEL_ONE = 0.03125
RIDGES = len(HERITABILITY)
LANES = 128
SUBLANES = 8
TILE = 256
WIDE = 512
ORDER = (12, 6, 10, 3, 13, 5, 11, 2, 14, 4, 8, 15, 7, 9, 1)


def level_zero_kernel(
    dosage_hbm,
    eigvec_hbm,
    eigval_hbm,
    pheno_hbm,
    place,
    *rest,
):
    count = len(rest) - 10
    outs_hbm, scratch = rest[:count], rest[count:]
    level_zero_body(dosage_hbm, eigvec_hbm, eigval_hbm, pheno_hbm, place, outs_hbm, *scratch)


def level_zero_body(
    dosage_hbm,
    eigvec_hbm,
    eigval_hbm,
    pheno_hbm,
    place,
    outs_hbm,
    dosage,
    eigvec,
    eigval,
    pheno,
    covariance,
    squares,
    scaled,
    slope,
    predicted,
    sems,
):
    samples, width = dosage.shape
    traits = pheno.shape[1]
    chunks = width // TILE
    copies = [
        pltpu.make_async_copy(
            dosage_hbm.at[:, pl.ds(c * TILE, TILE)], dosage.at[:, pl.ds(c * TILE, TILE)], sems.at[c]
        )
        for c in range(chunks)
    ]
    cases_copy = pltpu.make_async_copy(pheno_hbm, pheno, sems.at[chunks])
    basis = pltpu.make_async_copy(eigvec_hbm, eigvec, sems.at[chunks + 1])
    values = pltpu.make_async_copy(eigval_hbm, eigval, sems.at[chunks + 2])
    cases_copy.start()
    for copy in copies:
        copy.start()
    basis.start()
    values.start()

    row = lax.broadcasted_iota(jnp.int32, (traits, traits), 0)
    column = lax.broadcasted_iota(jnp.int32, (traits, traits), 1)
    cases_copy.wait()
    turned = lax.dot_general(
        jnp.where(row == column, 1.0, 0.0).astype(jnp.bfloat16),
        pheno[...],
        (((1,), (1,)), ((), ())),
        preferred_element_type=jnp.float32,
    )
    cases = jnp.sum(turned, axis=1, keepdims=True)
    center = cases / samples
    spread = jnp.sqrt(
        (cases * samples - cases * cases) / (samples * float(samples)) + EPSILON
    )
    ones = ((1.0 - center) / spread).astype(jnp.bfloat16).astype(jnp.float32)
    zeros = ((0.0 - center) / spread).astype(jnp.bfloat16).astype(jnp.float32)
    delta = ones - zeros
    left = jnp.concatenate([turned, jnp.ones((2 * SUBLANES, samples), jnp.float32)], axis=0).astype(
        jnp.bfloat16
    )
    for c in range(chunks):
        copies[c].wait()
        part = dosage[:, c * TILE : (c + 1) * TILE]
        covariance[:, c * TILE : (c + 1) * TILE] = jnp.dot(
            left, part, preferred_element_type=jnp.float32
        )
        square = part * part
        rows = samples
        while rows > 4 * SUBLANES:
            rows //= 2
            square = square[:rows] + square[rows : 2 * rows]
        squares[:, c * TILE : (c + 1) * TILE] = jnp.sum(
            square.astype(jnp.float32), axis=0, keepdims=True
        )
    total = covariance[traits : traits + 1, :]
    mean = total / samples
    deviation = jnp.sqrt(
        (squares[...] * samples - total * total) / (samples * float(samples)) + EPSILON
    )
    inverse = 1.0 / deviation
    cross = (
        (covariance[:traits, :] - cases * mean) * delta * inverse
    ).astype(jnp.bfloat16)
    basis.wait()
    values.wait()
    rotated = jnp.dot(cross, eigvec[...], preferred_element_type=jnp.float32)
    for r, value in enumerate(HERITABILITY):
        shrunk = rotated * (1.0 / (eigval[...] + width * (1.0 - value) / value))
        for g in range(traits // SUBLANES):
            start = (g * RIDGES + r) * SUBLANES
            scaled[start : start + SUBLANES, :] = shrunk[
                g * SUBLANES : (g + 1) * SUBLANES
            ].astype(jnp.bfloat16)
    for c in range(chunks):
        ridge = lax.dot_general(
            scaled[...],
            eigvec[c * TILE : (c + 1) * TILE, :],
            (((1,), (1,)), ((), ())),
            preferred_element_type=jnp.float32,
        )
        slope[:, c * TILE : (c + 1) * TILE] = (
            ridge * inverse[:, c * TILE : (c + 1) * TILE]
        ).astype(jnp.bfloat16)
    high = mean.astype(jnp.bfloat16).astype(jnp.float32)
    low = (mean - high).astype(jnp.bfloat16).astype(jnp.float32)
    rest = mean - high - low
    line = lax.broadcasted_iota(jnp.int32, (2 * SUBLANES, width), 0)
    means = jnp.where(line == 0, high, jnp.where(line == 1, low, jnp.where(line == 2, rest, 0.0)))
    offset = jnp.sum(
        lax.dot_general(
            slope[...],
            means.astype(jnp.bfloat16),
            (((1,), (1,)), ((), ())),
            preferred_element_type=jnp.float32,
        ),
        axis=1,
        keepdims=True,
    )
    outs = []
    for n in range(samples // WIDE):
        found = lax.dot_general(
            slope[...],
            dosage[n * WIDE : (n + 1) * WIDE, :],
            (((1,), (1,)), ((), ())),
            preferred_element_type=jnp.float32,
        )
        predicted[:, n * WIDE : (n + 1) * WIDE] = (found - offset).astype(jnp.bfloat16)
        for i, out in enumerate(outs_hbm):
            height = out.shape[0]
            first = 0
            if len(outs_hbm) > 1:
                first = pl.multiple_of((place[0] ^ i) * height, height)
            copy = pltpu.make_async_copy(
                predicted.at[pl.ds(first, height), pl.ds(n * WIDE, WIDE)],
                out.at[:, pl.ds(n * WIDE, WIDE)],
                sems.at[chunks + 3 + n * len(outs_hbm) + i],
            )
            copy.start()
            outs.append(copy)
    for copy in outs:
        copy.wait()


def level_zero(dosage, eigvec, eigval, pheno, place, heights):
    samples, width = dosage.shape
    traits = pheno.shape[1]
    rows = RIDGES * traits
    anywhere = pl.BlockSpec(memory_space=pl.ANY)
    copies = width // TILE + 3 + len(heights) * (samples // WIDE)
    return pl.pallas_call(
        level_zero_kernel,
        out_shape=[jax.ShapeDtypeStruct((height, samples), jnp.bfloat16) for height in heights],
        in_specs=[anywhere] * 4 + [pl.BlockSpec(memory_space=pltpu.SMEM)],
        out_specs=[anywhere] * len(heights),
        scratch_shapes=[
            pltpu.VMEM((samples, width), jnp.bfloat16),
            pltpu.VMEM((width, width), jnp.bfloat16),
            pltpu.VMEM((1, width), jnp.float32),
            pltpu.VMEM((samples, traits), jnp.bfloat16),
            pltpu.VMEM((traits + 2 * SUBLANES, width), jnp.float32),
            pltpu.VMEM((1, width), jnp.float32),
            pltpu.VMEM((rows, width), jnp.bfloat16),
            pltpu.VMEM((rows, width), jnp.bfloat16),
            pltpu.VMEM((rows, samples), jnp.bfloat16),
            pltpu.SemaphoreType.DMA((copies,)),
        ],
        compiler_params=pltpu.CompilerParams(vmem_limit_bytes=63 << 20),
        name="level_zero",
    )(dosage, eigvec, eigval, pheno, place)


def reorder_matrix(traits, blocks, parts):
    size = blocks * RIDGES * traits // parts
    row = lax.broadcasted_iota(jnp.int32, (size, size), 0)
    column = lax.broadcasted_iota(jnp.int32, (size, size), 1)
    group = blocks // parts
    block, rest = row % group, row // group
    ridge, pair = rest % RIDGES, rest // RIDGES
    trait = (pair % 2) * (traits // 2) + pair // 2
    return jnp.where(column == (block * RIDGES + ridge) * traits + trait, 1.0, 0.0).astype(
        jnp.bfloat16
    )


def inverse_two(m):
    (a, b), (c, d) = m
    scale = 1.0 / (a * d - b * c)
    return ((d * scale, -b * scale), (-c * scale, a * scale))


def product(x, y):
    return tuple(
        tuple(x[i][0] * y[0][j] + x[i][1] * y[1][j] for j in range(2)) for i in range(2)
    )


def negative(x):
    return tuple(tuple(-value for value in row) for row in x)


def inverse_four(m):
    def corner(i, j):
        return ((m[i][j], m[i][j + 1]), (m[i + 1][j], m[i + 1][j + 1]))

    first = inverse_two(corner(0, 0))
    left = product(corner(2, 0), first)
    right = product(first, corner(0, 2))
    inner = product(left, corner(0, 2))
    last = corner(2, 2)
    second = inverse_two(
        tuple(tuple(last[i][j] - inner[i][j] for j in range(2)) for i in range(2))
    )
    below = product(second, left)
    back = product(right, below)
    top = tuple(tuple(first[i][j] + back[i][j] for j in range(2)) for i in range(2))
    beside, below = negative(product(right, second)), negative(below)
    return [list(top[i]) + list(beside[i]) for i in range(2)] + [
        list(below[i]) + list(second[i]) for i in range(2)
    ]


def gather_lanes(tile, lanes):
    return jnp.take_along_axis(tile, lanes, axis=1)


def solve(table, span):
    heights, tiles = len(table), len(table[0])
    size = (tiles - 1) * SUBLANES
    lane = lax.broadcasted_iota(jnp.int32, (SUBLANES, LANES), 1)
    within = lane % span

    def eliminate(k, rows, count):
        home, low = k // span, k % span
        first, sub = k // SUBLANES, k % SUBLANES
        pivot = [
            [
                jnp.broadcast_to(rows[m][0][sub + n : sub + n + 1], (SUBLANES, LANES))
                for n in range(4)
            ]
            for m in range(count)
        ]
        inverse = inverse_four(pivot[:4])

        def combine(values):
            return [
                (values[0] * inverse[0][n] + values[1] * inverse[1][n])
                + (values[2] * inverse[2][n] + values[3] * inverse[3][n])
                for n in range(4)
            ]

        def clear(base, factors, r):
            return (
                base
                - (factors[0] * rows[0][r] + factors[1] * rows[1][r])
                - (factors[2] * rows[2][r] + factors[3] * rows[3][r])
            )

        later = []
        for m in range(4, count):
            factors = combine(pivot[m])
            later.append([clear(rows[m][r], factors, r) for r in range(tiles - first)])
        chosen = (within >= low) & (within < low + 4)
        for h in sorted(range(heights), key=lambda h: h != min(k + 4, size - 4) // span):
            factors = combine(
                [
                    jnp.broadcast_to(table[h][first][sub + m : sub + m + 1], (SUBLANES, LANES))
                    for m in range(4)
                ]
            )
            if h == home:
                for n in range(4):
                    for m in range(4):
                        factors[n] = jnp.where(within == low + m, -inverse[m][n], factors[n])
            for r in range(first, tiles):
                base = table[h][r]
                if h == home:
                    base = jnp.where(chosen, 0.0, base)
                table[h][r] = clear(base, factors, r - first)
        return later

    for k in range(0, size, 8):
        lanes = (lane - within) + k % span
        rows = [
            [gather_lanes(table[k // span][r], lanes + m) for r in range(k // SUBLANES, tiles)]
            for m in range(8)
        ]
        eliminate(k + 4, eliminate(k, rows, 8), 4)
    return [table[h][tiles - 1] for h in range(heights)]


def exchange(tiles, span):
    lane = lax.broadcasted_iota(jnp.int32, (SUBLANES, LANES), 1)
    tiles = list(tiles)
    for bit in (1, 2):
        shift = bit * span
        odd = (lane // shift) % 2 == 1
        for i in range(4):
            if not i & bit:
                x, y = tiles[i], tiles[i | bit]
                tiles[i] = jnp.where(odd, pltpu.roll(y, shift, 1), x)
                tiles[i | bit] = jnp.where(odd, y, pltpu.roll(x, LANES - shift, 1))
    return tiles


def newton_kernel(traits, blocks, place, *rest):
    *given, target, out, design, lhs = rest
    arrays = [given[0]] + [given[1 + ORDER.index(j)] for j in range(1, blocks)]
    samples = target.shape[1]
    predictors = RIDGES * blocks
    half = traits // 2
    parts = 2
    order = reorder_matrix(traits, blocks, parts)
    group = blocks // parts
    for part in range(parts):
        arrived = jnp.concatenate(
            [block[...] for block in arrays[part * group : (part + 1) * group]], axis=0
        )
        moved = jnp.dot(order, arrived, preferred_element_type=jnp.float32)
        for i in range(arrived.shape[0] // group):
            start = i * blocks + part * group
            design[start : start + group, :] = moved[i * group : (i + 1) * group].astype(
                jnp.bfloat16
            )
    level_ridge = LEVEL_ONE * samples
    lane = lax.broadcasted_iota(jnp.int32, (SUBLANES, LANES), 1)
    sub = lax.broadcasted_iota(jnp.int32, (SUBLANES, LANES), 0)
    upper = lane >= predictors
    pheno = target[...]
    middle = predictors + 2 * traits
    rows = predictors // SUBLANES

    def systems(weights):
        if weights is None:
            resid = pheno - 0.5
        else:
            spread_out = [
                jnp.where((lane // predictors) * half + s == sub, w, 0.0).astype(jnp.bfloat16)
                for s, w in enumerate(exchange(weights, blocks))
            ]
            logits = jnp.dot(
                jnp.concatenate(spread_out, axis=1), design[...], preferred_element_type=jnp.float32
            )
            prob = 1.0 / (1.0 + jnp.exp(-logits))
            curve = prob * (1.0 - prob)
            resid = pheno - prob
        resid = jnp.concatenate([resid, jnp.zeros_like(resid)], axis=0).astype(jnp.bfloat16)
        found = []
        for s in range(half):
            base = s * 2 * predictors
            pair = design[base : base + 2 * predictors, :]
            lhs[s, predictors:middle, :] = resid
            for start, trait, place in ((0, s, 0), (predictors, s + half, middle)):
                own = design[base + start : base + start + predictors, :]
                if weights is not None:
                    own = (own.astype(jnp.float32) * curve[trait : trait + 1, :]).astype(
                        jnp.bfloat16
                    )
                lhs[s, place : place + predictors, :] = own
            result = lax.dot_general(
                lhs[s], pair, (((1,), (1,)), ((), ())), preferred_element_type=jnp.float32
            )
            tiles = [
                jnp.where(
                    upper,
                    result[middle + SUBLANES * r : middle + SUBLANES * (r + 1)],
                    result[SUBLANES * r : SUBLANES * (r + 1)],
                )
                for r in range(rows)
            ]
            if weights is None:
                tiles = [tile * 0.25 for tile in tiles]
            first, second = predictors + s, predictors + s + half
            gradient = jnp.where(upper[:1], result[second : second + 1], result[first : first + 1])
            tiles.append(jnp.broadcast_to(gradient, (SUBLANES, LANES)))
            found.append(tiles)
        table = [[] for _ in range(RIDGES)]
        for r in range(rows + 1):
            for h, tile in enumerate(exchange([found[s][r] for s in range(half)], blocks)):
                if r < rows:
                    same = SUBLANES * r + sub == h * blocks + lane % blocks
                    tile = tile + jnp.where(same, level_ridge, 0.0)
                elif weights is not None:
                    tile = tile - level_ridge * weights[h]
                table[h].append(tile)
        return table

    table = systems(None)
    weights = tuple(jnp.zeros((SUBLANES, LANES), jnp.float32) for _ in range(RIDGES))
    for index in range(NEWTON):
        solved = solve(table, blocks)
        weights = tuple(
            weights[h] + jnp.broadcast_to(solved[h][0:1], (SUBLANES, LANES))
            for h in range(RIDGES)
        )
        if index < NEWTON - 1:
            table = systems(weights)
    result = jnp.zeros((SUBLANES, LANES), jnp.float32)
    for s, tile in enumerate(exchange(weights, blocks)):
        result = jnp.where(sub == s, tile, result)
        result = jnp.where(sub == s + half, pltpu.roll(tile, predictors, 1), result)
    block = lane % blocks
    result = gather_lanes(result, (lane - block) + (block ^ place[0]))
    out[...] = result[:, :predictors]


def newton(place, arrays, target, blocks):
    samples = target.shape[1]
    traits = target.shape[0]
    predictors = RIDGES * blocks
    inside = pl.BlockSpec(memory_space=pltpu.VMEM)
    return pl.pallas_call(
        functools.partial(newton_kernel, traits, blocks),
        out_shape=jax.ShapeDtypeStruct((traits, predictors), jnp.float32),
        in_specs=[pl.BlockSpec(memory_space=pltpu.SMEM)] + [inside] * (len(arrays) + 1),
        out_specs=inside,
        scratch_shapes=[
            pltpu.VMEM((traits * predictors, samples), jnp.bfloat16),
            pltpu.VMEM((traits // 2, 2 * predictors + 2 * traits, samples), jnp.bfloat16),
        ],
        compiler_params=pltpu.CompilerParams(vmem_limit_bytes=48 << 20),
        name="newton",
    )(place, *arrays, target)


def fetch_kernel(block, out):
    out[...] = block[...]


def fetch(block):
    inside = pl.BlockSpec(memory_space=pltpu.VMEM)
    return pl.pallas_call(
        fetch_kernel,
        out_shape=jax.ShapeDtypeStruct(block.shape, block.dtype),
        in_specs=[inside],
        out_specs=inside,
        cost_estimate=pl.CostEstimate(
            flops=0, bytes_accessed=4 * block.size, transcendentals=0
        ),
        compiler_params=pltpu.CompilerParams(vmem_limit_bytes=2 << 20),
        name="fetch",
    )(block)


def fit_traits(arrived, target):
    rows, samples = arrived.shape
    count = target.shape[0]
    predictors = rows // count
    design = arrived.reshape(-1, RIDGES, count, samples).transpose(2, 0, 1, 3)
    design = design.reshape(count, predictors, samples)
    level_ridge = LEVEL_ONE * samples
    weights = jnp.zeros((count, predictors), jnp.float32)
    identity = jnp.eye(predictors, dtype=jnp.float32)
    for _ in range(NEWTON):
        logits = jnp.einsum(
            "kqn,kq->kn", design, weights.astype(jnp.bfloat16), preferred_element_type=jnp.float32
        )
        prob = jax.nn.sigmoid(logits)
        resid = (target - prob).astype(jnp.bfloat16)
        weighted = (design * (prob * (1.0 - prob))[:, None, :]).astype(jnp.bfloat16)
        gram = jnp.einsum("kqn,kpn->kqp", weighted, design, preferred_element_type=jnp.float32)
        grad = jnp.einsum("kqn,kn->kq", design, resid, preferred_element_type=jnp.float32)
        grad = grad - level_ridge * weights
        factor = jnp.linalg.cholesky(gram + level_ridge * identity)
        partial_solve = lax.linalg.triangular_solve(
            factor, grad[:, :, None], left_side=True, lower=True
        )
        update = lax.linalg.triangular_solve(
            factor, partial_solve, left_side=True, lower=True, transpose_a=True
        )
        weights = weights + update[:, :, 0]
    return weights.reshape(count, -1, RIDGES).swapaxes(1, 2).reshape(count, predictors)


def on_device(dosage, eigvec, eigval, pheno):
    samples = dosage.shape[0]
    traits = pheno.shape[1]
    regions = lax.axis_size("region")
    per_device = traits // regions
    rows = RIDGES * per_device
    position = lax.axis_index("region")
    place = position.astype(jnp.int32).reshape(1)
    target = lax.dynamic_slice_in_dim(pheno, position * per_device, per_device, 1)
    target = target.astype(jnp.float32).T
    if per_device == SUBLANES and regions == len(ORDER) + 1:
        own, *arrays = level_zero(dosage, eigvec, eigval, pheno, place, [rows] * regions)
        arrays = [
            lax.ppermute(arrays[j - 1], "region", [(i, i ^ j) for i in range(regions)])
            for j in ORDER
        ]
        return newton(place, [fetch(own)] + arrays, target, regions)
    (predicted,) = level_zero(dosage, eigvec, eigval, pheno, place, [RIDGES * traits])
    predicted = predicted.reshape(-1, RIDGES, SUBLANES // per_device, per_device, samples)
    predicted = predicted.swapaxes(1, 2).reshape(RIDGES * traits, samples)
    arrived = lax.all_to_all(predicted, "region", split_axis=0, concat_axis=0, tiled=True)
    return fit_traits(arrived, target)


def solution(mesh):
    return jax.shard_map(
        on_device,
        mesh=mesh,
        in_specs=(
            P("cohort", "region"),
            P("region", "cohort"),
            P("cohort", "region"),
            P("cohort", None),
        ),
        out_specs=P("region", "cohort"),
        check_vma=False,
    )
```
